1024 devices in a mesh: dp: 8 (over x, core), ctx: 16 (over z), rep: 8 (over y).
Axes of the slice: x: 4, y: 8, z: 16, core: 2. Of those that a mesh axis runs over, the one named last changes fastest.
Arguments:
- inputs: bfloat16 [8, 16384, 4096], P('dp', ('ctx', 'rep')), may hold values from -24 to 24
- queries: bfloat16 [8, 16384, 2048], P('dp', ('ctx', 'rep')), may hold values from -24 to 24
- keys: bfloat16 [8, 16384, 512], P('dp', ('ctx', 'rep')), may hold values from -24 to 24
- values: bfloat16 [8, 16384, 512], P('dp', ('ctx', 'rep')), may hold values from -6 to 6
- grad_out: bfloat16 [8, 16384, 2048], P('dp', ('ctx', 'rep')), may hold values from -0.01953125 to 0.01953125
- doc_ids: int32 [8, 16384], P('dp', ('ctx', 'rep')), may hold values from 0 to 511, never falling along the last dimension, each value on 1 to 128 neighbouring positions
- plan: int32 [8, 512], P('dp', ('ctx', 'rep')), may hold values from 0 to 7, as said below
Outputs:
- placed_out: bfloat16 [8, 16384, 2048], P('dp', ('ctx', 'rep'))
- weight_grad: float32 [4096, 512], P('ctx')
The draws below stay inside these ranges and needn't reach their ends.
Inputs may be any that keep to these rules, and one draw needn't show every extreme that they name: `doc_ids`: ids never fall along a micro-batch; a document holds at most 128 positions. `plan`: for one sequence shard, the 4 blocks of a micro-batch go to 4 different micro-batches (itself possibly), and every micro-batch receives exactly one block of each local block index.
All inputs are finite; a program needn't handle non-finite values.
Results may differ from the reference program's by a relative error of at most 0.017.
Values may be sent and summed in bfloat16 or wider, within the bound.
A program may use at most 32 MiB of HBM per device.

```python
import math
import jax
import jax.numpy as jnp
import numpy as np
from jax import lax

D = 4096
HEAD_DIM = 128
Q_HEADS = 16
KV_HEADS = 4
GROUP = 4
TOK_DEV = 128
BLK_DEV = 4
BLOCK = 32
OWNERS = 8
SHARDS = 128
BATCHES = 8
SEQ = 16384
DOCS = 512
DEVICES = 1024


def paired_rows(key):
    base_q = jax.random.normal(jax.random.fold_in(key, 101), (BATCHES, SEQ, Q_HEADS * HEAD_DIM), jnp.float32)
    base_k = jax.random.normal(jax.random.fold_in(key, 102), (BATCHES, SEQ, KV_HEADS * HEAD_DIM), jnp.float32)
    base_q = jnp.clip(base_q, -4.5, 4.5)
    base_k = jnp.clip(base_k, -4.5, 4.5)
    return (base_q, base_k)


def draw_queries(key, part):
    return paired_rows(key)[0].astype(jnp.bfloat16)


def draw_keys(key, part):
    return paired_rows(key)[1].astype(jnp.bfloat16)


def draw_plan(key, part):
    groups = SHARDS
    offset_keys = jax.random.split(jax.random.fold_in(key, 201), groups)
    label_keys = jax.random.split(jax.random.fold_in(key, 202), groups)
    offsets = jax.vmap(lambda one_key: jax.random.permutation(one_key, OWNERS)[:BLK_DEV])(offset_keys)
    labels = jax.vmap(lambda one_key: jax.random.permutation(one_key, OWNERS))(label_keys)
    inverse = jnp.argsort(labels, axis=1)
    target = (inverse[:, :, None] + offsets[:, None, :]) % OWNERS
    chosen = jnp.take_along_axis(labels, target.reshape(groups, OWNERS * BLK_DEV), axis=1)
    chosen = chosen.reshape(SHARDS, OWNERS, BLK_DEV)
    chosen = jnp.transpose(chosen, (1, 0, 2)).reshape(BATCHES, SHARDS * BLK_DEV)
    return chosen.astype(jnp.int32)


def raised(result, key, source, target, shards_of, factor):
    owner, partner = [(jnp.arange(result.shape[dim]) // (result.shape[dim] // shards_of)).reshape([-1 if axis == dim else 1 for axis in range(result.ndim)]) for dim in (source, target)]
    chosen = jax.random.permutation(key, shards_of)[partner]
    strong = (owner == chosen) | (owner == (partner + shards_of // 2) % shards_of)
    return jnp.where(strong, factor * result, result)


def block_scale(stream_key, extent, shards, least, high):
    level = 1.0
    for axis_at, shards_of in shards:
        steps = jax.random.uniform(jax.random.fold_in(jax.random.fold_in(stream_key, 6), axis_at), (shards_of,), jnp.float32, least / len(shards), high / len(shards))
        level = level * jnp.repeat(jnp.exp(steps), extent[axis_at] // shards_of).reshape((-1,) + (1,) * (len(extent) - 1 - axis_at))
    return level


def profile(amount, total, reach, lean):
    loads = [(1 << 20) // math.isqrt(rank ** lean) + 1 for rank in range(2, amount + 1)]
    rest, given = total - reach - (amount - 1), [1] * (amount - 1)
    while rest > 0:
        free = [i for i in range(amount - 1) if given[i] < reach]
        whole, left = sum([loads[i] for i in free]), rest
        for i in free:
            addition = min(reach - given[i], max(1, left * loads[i] // whole), rest)
            given[i] = given[i] + addition
            rest = rest - addition
    return np.array([reach] + given)


def ragged_sizes(key, number_of, total, bound, slope):
    if number_of == 2:
        one = jax.random.randint(key, (), max(1, total - bound), min(bound, total - 1) + 1)
        return jnp.stack([one, total - one])
    sizes = jnp.asarray(profile(number_of, total, bound, slope), jnp.int32)
    twos = (number_of - 1) // 2
    source_of, receiver = sizes[1:1 + 2 * twos:2], sizes[2:2 + 2 * twos:2]
    room = jnp.minimum(source_of - 1, bound - receiver)
    moved = jax.random.randint(jax.random.fold_in(key, 1), (twos,), 0, 1 << 20) % (room + 1)
    sizes = sizes.at[1:1 + 2 * twos:2].set(source_of - moved).at[2:2 + 2 * twos:2].set(receiver + moved)
    return sizes[jax.random.permutation(jax.random.fold_in(key, 2), number_of)]


def centred(key, shape, width, bound, shards=(), held_as=jnp.bfloat16):
    entries = jax.random.normal(key, shape, jnp.float32) * width
    if len(shards) > 0:
        entries = block_scale(key, shape, shards, -0.22, 0.18) * entries
    return jnp.clip(entries, min=-bound, max=bound).astype(held_as)


def noise_with(stream_key, shape, width, most, cuts, heavy, held_as=jnp.bfloat16):
    entries = width * jax.random.normal(stream_key, shape, jnp.float32)
    if cuts:
        entries = entries * block_scale(stream_key, shape, cuts, -0.22, 0.18)
    return jnp.clip(raised(entries, jax.random.fold_in(stream_key, 3), *heavy), -most, most).astype(held_as)


def setup_inputs(seed: int = 0) -> dict:
    key_of = jax.random.split(jax.random.key(seed), 8)
    return {
        "inputs": noise_with(key_of[0], (BATCHES, SEQ, D), 1.0, 24.0, ((0, 8), (1, 128)), (1, 2, 128, 5.5)),
        "queries": draw_queries(jax.random.fold_in(key_of[7], 71), 0),
        "keys": draw_keys(jax.random.fold_in(key_of[7], 71), 0),
        "values": centred(key_of[3], (BATCHES, SEQ, KV_HEADS * HEAD_DIM), 1.0, 6.0, ((0, 8), (1, 128))),
        "grad_out": centred(key_of[4], (BATCHES, SEQ, Q_HEADS * HEAD_DIM), (0.5 / (TOK_DEV * DEVICES) ** 0.5), 0.01953125, ((0, 8), (1, 128))),
        "doc_ids": jax.vmap(lambda own: jnp.searchsorted(jnp.cumsum(ragged_sizes(own, DOCS, SEQ, TOK_DEV, 2)), jnp.arange(SEQ), side="right"))(jax.random.split(key_of[5], BATCHES)).reshape((BATCHES, SEQ)).astype(jnp.int32),
        "plan": draw_plan(jax.random.fold_in(key_of[7], 71), 0),
    }


def shard_weights(query_rows, key_rows, query_docs, key_docs, query_pos, key_pos):
    count_q = query_rows.shape[0]
    count_k = key_rows.shape[0]
    queries4 = query_rows.astype(jnp.float32).reshape(count_q, KV_HEADS, GROUP, HEAD_DIM)
    keys3 = key_rows.astype(jnp.float32).reshape(count_k, KV_HEADS, HEAD_DIM)
    scores = jnp.einsum('tgrd,ugd->grtu', queries4, keys3) * (1.0 / math.sqrt(HEAD_DIM))
    allowed = (query_docs[:, None] == key_docs[None, :]) & (key_pos[None, :] <= query_pos[:, None])
    scores = jnp.where(allowed, scores, -jnp.inf)
    row_max = lax.optimization_barrier(jnp.max(scores, axis=-1, keepdims=True))
    exponent = jnp.exp(scores - row_max)
    row_sum = lax.optimization_barrier(jnp.sum(exponent, axis=-1, keepdims=True))
    return (exponent / row_sum).astype(jnp.bfloat16)

def reference(inputs, queries, keys, values, grad_out, doc_ids, plan):
    q_width = Q_HEADS * HEAD_DIM
    kv_width = KV_HEADS * HEAD_DIM

    def per_batch(grad_sum, batch):
        batch_inputs, batch_queries, batch_keys, batch_values, batch_grads, batch_docs = batch
        keys_pad = jnp.concatenate([jnp.zeros((TOK_DEV, kv_width), batch_keys.dtype), batch_keys], 0)
        values_pad = jnp.concatenate([jnp.zeros((TOK_DEV, kv_width), batch_values.dtype), batch_values], 0)
        docs_pad = jnp.concatenate([jnp.full((TOK_DEV,), -1, jnp.int32), batch_docs], 0)

        def per_shard(shard_index):
            first = shard_index * TOK_DEV
            query_rows = lax.dynamic_slice_in_dim(batch_queries, first, TOK_DEV, 0)
            grad_rows = lax.dynamic_slice_in_dim(batch_grads, first, TOK_DEV, 0)
            query_docs = lax.dynamic_slice_in_dim(batch_docs, first, TOK_DEV, 0)
            key_rows = lax.dynamic_slice_in_dim(keys_pad, first, 2 * TOK_DEV, 0)
            value_rows = lax.dynamic_slice_in_dim(values_pad, first, 2 * TOK_DEV, 0)
            key_docs = lax.dynamic_slice_in_dim(docs_pad, first, 2 * TOK_DEV, 0)
            query_pos = first + jnp.arange(TOK_DEV, dtype=jnp.int32)
            key_pos = first - TOK_DEV + jnp.arange(2 * TOK_DEV, dtype=jnp.int32)
            probabilities = shard_weights(query_rows, key_rows, query_docs, key_docs, query_pos, key_pos)
            weights32 = probabilities.astype(jnp.float32)
            values3 = value_rows.astype(jnp.float32).reshape(2 * TOK_DEV, KV_HEADS, HEAD_DIM)
            attended = jnp.einsum('grtu,ugd->tgrd', weights32, values3).astype(jnp.bfloat16).reshape(TOK_DEV, q_width)
            grads4 = grad_rows.astype(jnp.float32).reshape(TOK_DEV, KV_HEADS, GROUP, HEAD_DIM)
            value_grad = jnp.einsum('grtu,tgrd->ugd', weights32, grads4).reshape(2 * TOK_DEV, kv_width)
            return (attended, value_grad)
        attended, value_grad = lax.map(per_shard, jnp.arange(SHARDS, dtype=jnp.int32))
        own_part = value_grad[:, TOK_DEV:]
        later_part = jnp.concatenate([value_grad[1:, :TOK_DEV], jnp.zeros((1, TOK_DEV, kv_width), value_grad.dtype)], 0)
        grad_values = (own_part + later_part).astype(jnp.bfloat16)

        def per_term(running, pair):
            shard_inputs, shard_grads = pair
            term = jnp.dot(shard_inputs.T, shard_grads, preferred_element_type=jnp.float32)
            rounded = lax.optimization_barrier(term.astype(jnp.bfloat16)).astype(jnp.float32)
            return (running + rounded, None)
        grad_sum, unused = lax.scan(per_term, grad_sum, (batch_inputs.reshape(SHARDS, TOK_DEV, D), grad_values))
        return (grad_sum, attended.reshape(SEQ, q_width))
    weight_grad, attended = lax.scan(per_batch, jnp.zeros((D, kv_width), jnp.float32), (inputs, queries, keys, values, grad_out, doc_ids))
    block_count = SHARDS * BLK_DEV
    pieces = attended.reshape(OWNERS, block_count, BLOCK, q_width)
    targets = plan.reshape(OWNERS, block_count).astype(jnp.int32)
    blk_index = jnp.broadcast_to(jnp.arange(block_count, dtype=jnp.int32)[None, :], targets.shape)
    placed = jnp.zeros_like(pieces).at[targets, blk_index].set(pieces)
    return (placed.reshape(BATCHES, SEQ, q_width), weight_grad)
```

```python
import math

import jax
import jax.numpy as jnp
from jax import lax
from jax.sharding import PartitionSpec as P

HEAD_DIM = 128
KV_HEADS = 4
GROUP = 4


def from_behind(value, axis, by):
    devices = lax.axis_size(axis)
    pairs = [(i, i + by) for i in range(devices) if 0 <= i + by < devices]
    return lax.ppermute(value, axis, pairs)


def block_attention(query_rows, key_rows, query_docs, key_docs, query_pos, key_pos):
    count_q = query_rows.shape[0]
    count_k = key_rows.shape[0]
    queries4 = query_rows.reshape(count_q, KV_HEADS, GROUP, HEAD_DIM)
    keys3 = key_rows.reshape(count_k, KV_HEADS, HEAD_DIM)
    scores = jnp.einsum("tgrd,ugd->grtu", queries4, keys3, preferred_element_type=jnp.float32) * (
        1.0 / math.sqrt(HEAD_DIM)
    )
    allowed = (query_docs[:, None] == key_docs[None, :]) & (key_pos[None, :] <= query_pos[:, None])
    scores = jnp.where(allowed, scores, -jnp.inf)
    row_max = jnp.max(scores, axis=-1, keepdims=True)
    exponent = jnp.exp(scores - row_max)
    row_sum = jnp.sum(exponent, axis=-1, keepdims=True)
    probabilities = (exponent / row_sum).astype(jnp.bfloat16)
    return (probabilities, row_max, row_sum)


def spread_inputs(input_rows):
    count_t, width = input_rows.shape
    ctx, dp = lax.axis_size("ctx"), lax.axis_size("dp")
    parts = input_rows.reshape(count_t, ctx, dp, width // (ctx * dp))
    parts = jnp.transpose(parts, (2, 0, 1, 3)).reshape(dp, count_t, width // dp)
    spread = lax.all_to_all(parts, "dp", split_axis=0, concat_axis=0, tiled=True)
    return spread.reshape(dp * count_t, width // dp)


def reduced_grad(spread_rows, grad_values):
    ctx, dp, rep = lax.axis_size("ctx"), lax.axis_size("dp"), lax.axis_size("rep")
    width = grad_values.shape[1]
    all_values = lax.all_gather(grad_values, "dp", axis=0, tiled=True)
    part = jnp.einsum("tc,tf->cf", spread_rows, all_values, preferred_element_type=jnp.float32)
    rows = part.shape[0] // (ctx * rep)
    part = part.astype(jnp.bfloat16).reshape(ctx, rep, rows, width)
    part = jnp.transpose(part, (1, 0, 2, 3)).reshape(rep, ctx * rows, width)
    part = lax.all_to_all(part, "rep", split_axis=0, concat_axis=0, tiled=True)
    part = jnp.sum(part.astype(jnp.float32), axis=0).astype(jnp.bfloat16)
    part = part.reshape(ctx, rows, width)
    part = lax.all_to_all(part, "ctx", split_axis=0, concat_axis=0, tiled=True)
    total = jnp.sum(part.astype(jnp.float32), axis=0)
    return lax.all_gather(total, ("dp", "rep"), axis=0, tiled=True)


def local(inputs, queries, keys, values, grad_out, doc_ids, plan):
    token_count = inputs.shape[1]
    q_width = queries.shape[2]
    kv_width = keys.shape[2]
    input_rows = inputs[0]
    query_rows = queries[0]
    key_rows = keys[0]
    value_rows = values[0]
    grad_rows = grad_out[0]
    row_docs = doc_ids[0]
    spread_rows = spread_inputs(input_rows)
    shard_index = lax.axis_index(("ctx", "rep"))
    query_pos = shard_index * token_count + jnp.arange(token_count, dtype=jnp.int32)
    prior_keys, prior_values, prior_docs = from_behind(
        (key_rows, value_rows, row_docs + 1), ("ctx", "rep"), 1
    )
    keys_all = jnp.concatenate([prior_keys, key_rows], 0)
    values_all = jnp.concatenate([prior_values, value_rows], 0)
    docs_all = jnp.concatenate([prior_docs - 1, row_docs], 0)
    pos_all = jnp.concatenate([query_pos - token_count, query_pos], 0)
    probabilities, row_max, row_sum = block_attention(
        query_rows, keys_all, row_docs, docs_all, query_pos, pos_all
    )
    values3 = values_all.reshape(2 * token_count, KV_HEADS, HEAD_DIM)
    attended = jnp.einsum(
        "grtu,ugd->tgrd", probabilities, values3, preferred_element_type=jnp.float32
    ).astype(jnp.bfloat16)
    attended = attended.reshape(token_count, q_width)
    owner_count = lax.axis_size("dp")
    block_count = plan.shape[1]
    block_rows = token_count // block_count
    targets = plan[0]
    owner_index = jnp.arange(owner_count, dtype=jnp.int32)
    chosen = owner_index[:, None] == targets[None, :]
    pieces = attended.reshape(block_count, block_rows, q_width)
    outgoing = jnp.einsum(
        "pi,ibf->pbf", chosen.astype(jnp.bfloat16), pieces, preferred_element_type=jnp.float32
    ).astype(jnp.bfloat16)
    block_labels = jnp.sum(
        chosen.astype(jnp.int32) * (jnp.arange(block_count, dtype=jnp.int32)[None, :] + 1),
        axis=1,
        keepdims=True,
    )
    arrived, arrived_labels = (
        lax.all_to_all(outgoing, "dp", split_axis=0, concat_axis=0, tiled=True),
        lax.all_to_all(block_labels, "dp", split_axis=0, concat_axis=0, tiled=True),
    )
    matched = arrived_labels[:, 0][None, :] == jnp.arange(block_count, dtype=jnp.int32)[:, None] + 1
    placed = jnp.einsum(
        "ip,pbf->ibf", matched.astype(jnp.bfloat16), arrived, preferred_element_type=jnp.float32
    ).astype(jnp.bfloat16)
    placed = placed.reshape(1, token_count, q_width)
    grads4 = grad_rows.reshape(token_count, KV_HEADS, GROUP, HEAD_DIM)
    value_grad = jnp.einsum(
        "grtu,tgrd->ugd", probabilities, grads4, preferred_element_type=jnp.float32
    )
    value_grad = value_grad.reshape(2 * token_count, kv_width)
    returned = from_behind(
        value_grad[:token_count].astype(jnp.bfloat16), ("ctx", "rep"), -1
    ).astype(jnp.float32)
    grad_values = (value_grad[token_count:] + returned).astype(jnp.bfloat16)
    weight_grad = reduced_grad(spread_rows, grad_values)
    return (placed, weight_grad)


def solution(mesh):
    in_specs = (
        P("dp", ("ctx", "rep"), None),
        P("dp", ("ctx", "rep"), None),
        P("dp", ("ctx", "rep"), None),
        P("dp", ("ctx", "rep"), None),
        P("dp", ("ctx", "rep"), None),
        P("dp", ("ctx", "rep")),
        P("dp", ("ctx", "rep")),
    )
    out_specs = (P("dp", ("ctx", "rep"), None), P("ctx", None))
    return jax.shard_map(local, mesh=mesh, in_specs=in_specs, out_specs=out_specs, check_vma=False)
```

```python
import math

import jax
import jax.numpy as jnp
from jax import lax
from jax.experimental import pallas as pl
from jax.experimental.pallas import tpu as pltpu
from jax.sharding import PartitionSpec as P

HEAD_DIM = 128
KV_HEADS = 4
GROUP = 4
LANES = 128
MESH = pl.DeviceIdType.MESH


def kernel(
    sizes,
    x_ref, q_ref, k_ref, v_ref, g_ref, docs_ref, plan_ref,
    placed_ref, wg_ref,
    perm, xs, xg, kprev, vprev, docprev, probs, dvp, dvo, dvr, gvg, att, slots, arr,
    planrow, planall, ysend, yown, yrecv, zf, zsend, zrecv, full,
    nb_s, nb_r, x_s, x_r, gv_s, gv_r, gf_s, gf_r, a_s, a_r, p_s, p_r,
    y_s, y_r, z_s, z_r, ay_s, ay_r, ad_s, ad_r,
):
    DP, C, R = sizes
    X = DP // 2
    T, D = x_ref.shape
    W = k_ref.shape[1]
    blocks = plan_ref.shape[1]
    brow = T // blocks
    U = D // (DP * C)
    JJ = U // R
    CC = LANES // U
    NB = C // CC
    CH = CC * JJ
    f32, bf16 = jnp.float32, jnp.bfloat16

    dp, ctx, rep = lax.axis_index("dp"), lax.axis_index("ctx"), lax.axis_index("rep")
    chip, core = dp // 2, dp % 2
    shard = ctx * R + rep
    after, before = (shard + 1) % (C * R), (shard + C * R - 1) % (C * R)
    next_dev = {"ctx": after // R, "rep": after % R}
    prev_dev = {"ctx": before // R, "rep": before % R}

    def dp_to(c, k):
        return ((chip + k) % X) * 2 + (core + c) % 2

    dp_peers = [(c, k) for c in range(2) for k in range(X) if (c, k) != (0, 0)]

    barrier = pltpu.get_barrier_semaphore()

    def greet(device):
        pl.semaphore_signal(barrier, inc=1, device_id=device, device_id_type=MESH)

    greet(next_dev)
    greet(prev_dev)
    for c, k in dp_peers:
        greet({"dp": dp_to(c, k)})
    for j in range(1, R):
        greet({"rep": (rep + j) % R})
    for j in range(1, C):
        greet({"ctx": (ctx + j) % C})

    def send(src, dst, ssem, rsem, device):
        copy = pltpu.make_async_remote_copy(
            src_ref=src, dst_ref=dst, send_sem=ssem, recv_sem=rsem, device_id=device, device_id_type=MESH
        )
        copy.start()
        return copy

    lane = lax.broadcasted_iota(jnp.int32, (1, LANES), 1)
    row = jnp.zeros((1, LANES), jnp.int32)
    for i in range(blocks):
        row = jnp.where(lane == i, plan_ref[0, i], row)
    planrow[...] = row

    width = CC * DP * U
    for d in range(DP):
        o = lax.broadcasted_iota(jnp.int32, (LANES, 1), 0)
        rr, cc, jj = o // CH, (o % CH) // JJ, o % JJ
        source = cc * (DP * U) + d * U + rr * JJ + jj
        column = lax.broadcasted_iota(jnp.int32, (LANES, width), 1)
        perm[d] = jnp.where(column == source, 1.0, 0.0).astype(bf16)

    pl.semaphore_wait(barrier, 2 + (DP - 1) + (R - 1) + (C - 1))

    pending = []
    near = [
        send(k_ref, kprev, nb_s.at[0], nb_r.at[0], next_dev),
        send(v_ref, vprev, nb_s.at[1], nb_r.at[1], next_dev),
        send(docs_ref, docprev, nb_s.at[2], nb_r.at[2], next_dev),
    ]

    for b in range(NB):
        for d in range(DP):
            xs[d, b * LANES:(b + 1) * LANES, :] = lax.dot_general(
                perm[d], x_ref[:, b * width:(b + 1) * width], (((1,), (1,)), ((), ())),
                preferred_element_type=f32,
            ).astype(bf16)
    x_copies, p_copies = {}, {}
    for c, k in dp_peers:
        to = {"dp": dp_to(c, k)}
        p_copies[c, k] = send(planrow, planall.at[c, k], p_s.at[c, k], p_r.at[c, k], to)
        x_copies[c, k] = send(xs.at[dp_to(c, k)], xg.at[c, k], x_s.at[c, k], x_r.at[c, k], to)
    xg[0, 0] = xs[dp]

    docs = docs_ref[...].astype(f32)
    by_row = jnp.broadcast_to(docs, (T, T)).T
    u_pos = lax.broadcasted_iota(jnp.int32, (T, T), 1)
    t_pos = lax.broadcasted_iota(jnp.int32, (T, T), 0)
    own = jnp.where((by_row == docs) & (u_pos <= t_pos), 1.0, 0.0)
    for copy in near:
        copy.wait()
    prior = jnp.where(by_row == docprev[...].astype(f32), 1.0, 0.0) * jnp.where(shard > 0, 1.0, 0.0)
    allowed = jnp.concatenate([prior, own], axis=1)
    allowed = jnp.concatenate([allowed] * GROUP, axis=0) > 0.5

    def heads(ref, g):
        return jnp.concatenate(
            [ref[:, (g * GROUP + h) * HEAD_DIM:(g * GROUP + h + 1) * HEAD_DIM] for h in range(GROUP)], axis=0
        )

    for g in range(KV_HEADS):
        cols = slice(g * HEAD_DIM, (g + 1) * HEAD_DIM)
        keys = jnp.concatenate([kprev[:, cols], k_ref[:, cols]], axis=0)
        scores = lax.dot_general(
            heads(q_ref, g), keys, (((1,), (1,)), ((), ())), preferred_element_type=f32
        ) * (1.0 / math.sqrt(HEAD_DIM))
        scores = jnp.where(allowed, scores, -jnp.inf)
        exponent = jnp.exp(scores - jnp.max(scores, axis=-1, keepdims=True))
        p = (exponent * (1.0 / jnp.sum(exponent, axis=-1, keepdims=True))).astype(bf16)
        probs[g] = p
        dv = lax.dot_general(p, heads(g_ref, g), (((0,), (0,)), ((), ())), preferred_element_type=f32)
        dvp[:, cols] = dv[:T].astype(bf16)
        dvo[:, cols] = dv[T:]
    dv_copy = send(dvp, dvr, nb_s.at[3], nb_r.at[3], prev_dev)

    for g in range(KV_HEADS):
        cols = slice(g * HEAD_DIM, (g + 1) * HEAD_DIM)
        vals = jnp.concatenate([vprev[:, cols], v_ref[:, cols]], axis=0)
        out = jnp.dot(probs[g], vals, preferred_element_type=f32).astype(bf16)
        for h in range(GROUP):
            att[:, (g * GROUP + h) * HEAD_DIM:(g * GROUP + h + 1) * HEAD_DIM] = out[h * T:(h + 1) * T]

    dv_copy.wait()
    gvg[0, 0] = (dvo[...] + dvr[...].astype(f32)).astype(bf16)
    gv_copies = {}
    for c, k in [(1, 0)] + [(0, k) for k in range(1, X)]:
        gv_copies[c, k] = send(gvg.at[0, 0], gvg.at[c, k], gv_s.at[c, k], gv_r.at[c, k], {"dp": dp_to(c, k)})

    for p in range(DP):
        slot = jnp.zeros((brow, att.shape[1]), bf16)
        for i in range(blocks):
            weight = jnp.where(plan_ref[0, i] == p, 1.0, 0.0).astype(f32)
            slot = slot + att[i * brow:(i + 1) * brow, :] * jnp.full((1, 1), weight, f32).astype(bf16)
        slots[p] = slot
    a_copies = {}
    for c, k in dp_peers:
        a_copies[c, k] = send(
            slots.at[dp_to(c, k)], arr.at[c, k], a_s.at[c, k], a_r.at[c, k], {"dp": dp_to(c, k)}
        )

    for k in range(1, X):
        gv_copies[0, k].wait_recv()
        gv_copies[1, k] = send(gvg.at[0, k], gvg.at[1, k], gf_s.at[k], gf_r.at[k], {"dp": dp_to(1, 0)})
    for c, k in dp_peers:
        x_copies[c, k].wait_recv()
    gv_copies[1, 0].wait_recv()
    for k in range(1, X):
        gv_copies[1, k].wait_recv()

    for b in range(NB):
        rows = slice(b * LANES, (b + 1) * LANES)
        part = jnp.zeros((LANES, W), f32)
        for c in range(2):
            for k in range(X):
                part = part + jnp.dot(xg[c, k, rows, :], gvg[c, k], preferred_element_type=f32)
        yown[b] = part
        for r in range(R):
            ysend[r, b * CH:(b + 1) * CH, :] = part[r * CH:(r + 1) * CH].astype(bf16)
    y_copies = [
        send(ysend.at[(rep + j) % R], yrecv.at[j], y_s.at[j], y_r.at[j], {"rep": (rep + j) % R})
        for j in range(1, R)
    ]
    for copy in y_copies:
        copy.wait_recv()
    for b in range(NB):
        total = yown[b, pl.ds(pl.multiple_of(rep * CH, CH), CH), :]
        for j in range(1, R):
            total = total + yrecv[j, b * CH:(b + 1) * CH, :].astype(f32)
        for cc in range(CC):
            for w in range(W // LANES):
                zf[b * CC + cc, w * JJ:(w + 1) * JJ, :] = total[
                    cc * JJ:(cc + 1) * JJ, w * LANES:(w + 1) * LANES
                ]
    zsend[...] = zf[...].astype(bf16)
    z_copies = [
        send(zsend.at[(ctx + j) % C], zrecv.at[j], z_s.at[j], z_r.at[j], {"ctx": (ctx + j) % C})
        for j in range(1, C)
    ]

    for c, k in dp_peers:
        p_copies[c, k].wait_recv()
        a_copies[c, k].wait_recv()
    arr[0, 0] = slots[dp]
    planall[0, 0] = planrow[...]
    for i in range(blocks):
        result = jnp.zeros((brow, att.shape[1]), bf16)
        for c in range(2):
            for k in range(X):
                weight = jnp.where(planall[c, k][:, i:i + 1] == dp, 1.0, 0.0).astype(bf16)
                result = result + arr[c, k] * weight
        placed_ref[i * brow:(i + 1) * brow, :] = result

    for copy in z_copies:
        copy.wait_recv()
    total = zf[ctx]
    for j in range(1, C):
        total = total + zrecv[j].astype(f32)
    full[dp, rep] = total
    ay_copies = [
        send(full.at[dp, rep], full.at[dp, rep], ay_s.at[j], ay_r.at[j], {"rep": (rep + j) % R})
        for j in range(1, R)
    ]
    for copy in ay_copies:
        copy.wait_recv()
    ad_copies = [
        send(full.at[dp], full.at[dp], ad_s.at[c, k], ad_r.at[c, k], {"dp": dp_to(c, k)}) for c, k in dp_peers
    ]
    for copy in ad_copies:
        copy.wait_recv()
    for d in range(DP):
        for r in range(R):
            for w in range(W // LANES):
                wg_ref[d * U + r * JJ:d * U + (r + 1) * JJ, w * LANES:(w + 1) * LANES] = full[
                    d, r, w * JJ:(w + 1) * JJ, :
                ]
    pending = [x_copies, p_copies, a_copies, gv_copies]
    for group in pending:
        for copy in group.values():
            copy.wait_send()
    for copy in y_copies + z_copies + ay_copies + ad_copies:
        copy.wait_send()


def local(inputs, queries, keys, values, grad_out, doc_ids, plan):
    DP, C, R = lax.axis_size("dp"), lax.axis_size("ctx"), lax.axis_size("rep")
    X = DP // 2
    T, D = inputs.shape[1:]
    QW, W = queries.shape[2], keys.shape[2]
    blocks = plan.shape[1]
    U = D // (DP * C)
    JJ, CC = U // R, LANES // U
    NB, rows = C // CC, C * U
    brow = T // blocks
    zrow = JJ * (W // LANES)
    bf16, f32, i32 = jnp.bfloat16, jnp.float32, jnp.int32
    vmem = pltpu.VMEM
    dma = pltpu.SemaphoreType.DMA
    spec = pl.BlockSpec(memory_space=pltpu.VMEM)

    def body(*refs):
        kernel((DP, C, R), *refs)

    placed, weight_grad = pl.pallas_call(
        body,
        out_shape=(jax.ShapeDtypeStruct((T, QW), bf16), jax.ShapeDtypeStruct((D // C, W), f32)),
        in_specs=[spec] * 6 + [pl.BlockSpec(memory_space=pltpu.SMEM)],
        out_specs=(spec, spec),
        scratch_shapes=[
            vmem((DP, LANES, CC * DP * U), bf16),
            vmem((DP, rows, T), bf16),
            vmem((2, X, rows, T), bf16),
            vmem((T, W), bf16),
            vmem((T, W), bf16),
            vmem((1, T), i32),
            vmem((KV_HEADS, GROUP * T, 2 * T), bf16),
            vmem((T, W), bf16),
            vmem((T, W), f32),
            vmem((T, W), bf16),
            vmem((2, X, T, W), bf16),
            vmem((T, QW), bf16),
            vmem((DP, brow, QW), bf16),
            vmem((2, X, brow, QW), bf16),
            vmem((1, LANES), i32),
            vmem((2, X, 1, LANES), i32),
            vmem((R, C * JJ, W), bf16),
            vmem((NB, LANES, W), f32),
            vmem((R, C * JJ, W), bf16),
            vmem((C, zrow, LANES), f32),
            vmem((C, zrow, LANES), bf16),
            vmem((C, zrow, LANES), bf16),
            vmem((DP, R, zrow, LANES), f32),
            dma((4,)), dma((4,)),
            dma((2, X)), dma((2, X)),
            dma((2, X)), dma((2, X)),
            dma((X,)), dma((X,)),
            dma((2, X)), dma((2, X)),
            dma((2, X)), dma((2, X)),
            dma((R,)), dma((R,)),
            dma((C,)), dma((C,)),
            dma((R,)), dma((R,)),
            dma((2, X)), dma((2, X)),
        ],
        compiler_params=pltpu.CompilerParams(
            collective_id=0, has_side_effects=True, vmem_limit_bytes=50 * 1024 * 1024
        ),
    )(inputs[0], queries[0], keys[0], values[0], grad_out[0], doc_ids, plan)
    return (placed[None], weight_grad)


def solution(mesh):
    tokens = P("dp", ("ctx", "rep"), None)
    marks = P("dp", ("ctx", "rep"))
    return jax.shard_map(
        local,
        mesh=mesh,
        in_specs=(tokens, tokens, tokens, tokens, tokens, marks, marks),
        out_specs=(tokens, P("ctx", None)),
        check_vma=False,
    )
```

```python
import math

import jax
import jax.numpy as jnp
from jax import lax
from jax.experimental import pallas as pl
from jax.experimental.pallas import tpu as pltpu
from jax.sharding import PartitionSpec as P

HEAD_DIM = 128
KV_HEADS = 4
GROUP = 4
LANES = 128
MESH = pl.DeviceIdType.MESH


def kernel(
    sizes,
    x_hbm, q_hbm, k_hbm, v_hbm, g_hbm, docs_ref, plan_ref,
    placed_hbm, wg_ref,
    placed_ref, x_ref, q_ref, k_ref, v_ref, g_ref, perm, xs, xg, kprev, vprev, docprev, probs, dvp, dvo, dvr, gvg, att, slots, arr,
    planrow, planall, ysend, yown, yrecv, zf, zsend, zrecv, full,
    nb_s, nb_r, x_s, x_r, gv_s, gv_r, gf_s, gf_r, a_s, a_r, p_s, p_r,
    y_s, y_r, z_s, z_r, ay_s, ay_r, ad_s, ad_r, in_s, out_s,
):
    DP, C, R = sizes
    X = DP // 2
    T, D = x_hbm.shape
    W = k_hbm.shape[1]
    blocks = plan_ref.shape[1]
    brow = T // blocks
    U = D // (DP * C)
    JJ = U // R
    CC = LANES // U
    NB = C // CC
    CH = CC * JJ
    f32, bf16 = jnp.float32, jnp.bfloat16

    dp, ctx, rep = lax.axis_index("dp"), lax.axis_index("ctx"), lax.axis_index("rep")
    chip, core = dp // 2, dp % 2
    shard = ctx * R + rep
    after, before = (shard + 1) % (C * R), (shard + C * R - 1) % (C * R)
    next_dev = {"ctx": after // R, "rep": after % R}
    prev_dev = {"ctx": before // R, "rep": before % R}

    def dp_to(c, k):
        return ((chip + k) % X) * 2 + (core + c) % 2

    dp_peers = [(c, k) for c in range(2) for k in range(X) if (c, k) != (0, 0)]

    barrier = pltpu.get_barrier_semaphore()

    def greet(device):
        pl.semaphore_signal(barrier, inc=1, device_id=device, device_id_type=MESH)

    greet(next_dev)
    greet(prev_dev)
    for c, k in dp_peers:
        greet({"dp": dp_to(c, k)})
    for j in range(1, R):
        greet({"rep": (rep + j) % R})
    for j in range(1, C):
        greet({"ctx": (ctx + j) % C})

    loads = [
        pltpu.make_async_copy(src, dst, in_s.at[i])
        for i, (src, dst) in enumerate(
            [(k_hbm, k_ref), (x_hbm, x_ref), (v_hbm, v_ref), (q_hbm, q_ref), (g_hbm, g_ref)]
        )
    ]
    for load in loads:
        load.start()

    def send(src, dst, ssem, rsem, device):
        copy = pltpu.make_async_remote_copy(
            src_ref=src, dst_ref=dst, send_sem=ssem, recv_sem=rsem, device_id=device, device_id_type=MESH
        )
        copy.start()
        return copy

    lane = lax.broadcasted_iota(jnp.int32, (1, LANES), 1)
    row = jnp.zeros((1, LANES), jnp.int32)
    for i in range(blocks):
        row = jnp.where(lane == i, plan_ref[0, i], row)
    planrow[...] = row

    width = CC * DP * U
    for d in range(DP):
        o = lax.broadcasted_iota(jnp.int32, (LANES, 1), 0)
        rr, cc, jj = o // CH, (o % CH) // JJ, o % JJ
        source = cc * (DP * U) + d * U + rr * JJ + jj
        column = lax.broadcasted_iota(jnp.int32, (LANES, width), 1)
        perm[d] = jnp.where(column == source, 1.0, 0.0).astype(bf16)

    for load in loads:
        load.wait()
    pl.semaphore_wait(barrier, 2 + (DP - 1) + (R - 1) + (C - 1))

    near = [
        send(k_ref, kprev, nb_s.at[0], nb_r.at[0], next_dev),
        send(docs_ref, docprev, nb_s.at[2], nb_r.at[2], next_dev),
    ]
    v_copy = send(v_ref, vprev, nb_s.at[1], nb_r.at[1], next_dev)

    for b in range(NB):
        for d in range(DP):
            xs[d, b * LANES:(b + 1) * LANES, :] = lax.dot_general(
                perm[d], x_ref[:, b * width:(b + 1) * width], (((1,), (1,)), ((), ())),
                preferred_element_type=f32,
            ).astype(bf16)
    x_copies, p_copies = {}, {}
    for c, k in dp_peers:
        to = {"dp": dp_to(c, k)}
        p_copies[c, k] = send(planrow, planall.at[c, k], p_s.at[c, k], p_r.at[c, k], to)
        x_copies[c, k] = send(xs.at[dp_to(c, k)], xg.at[c, k], x_s.at[c, k], x_r.at[c, k], to)
    xg[0, 0] = xs[dp]

    docs = docs_ref[...].astype(f32)
    by_row = jnp.broadcast_to(docs, (T, T)).T
    u_pos = lax.broadcasted_iota(jnp.int32, (T, T), 1)
    t_pos = lax.broadcasted_iota(jnp.int32, (T, T), 0)
    own = jnp.where((by_row == docs) & (u_pos <= t_pos), 1.0, 0.0)
    for copy in near:
        copy.wait()
    prior = jnp.where(by_row == docprev[...].astype(f32), 1.0, 0.0) * jnp.where(shard > 0, 1.0, 0.0)
    allowed = jnp.concatenate([prior, own], axis=1)
    allowed = jnp.concatenate([allowed] * GROUP, axis=0) > 0.5

    def heads(ref, g):
        return jnp.concatenate(
            [ref[:, (g * GROUP + h) * HEAD_DIM:(g * GROUP + h + 1) * HEAD_DIM] for h in range(GROUP)], axis=0
        )

    for g in range(KV_HEADS):
        cols = slice(g * HEAD_DIM, (g + 1) * HEAD_DIM)
        keys = jnp.concatenate([kprev[:, cols], k_ref[:, cols]], axis=0)
        scores = lax.dot_general(
            heads(q_ref, g), keys, (((1,), (1,)), ((), ())), preferred_element_type=f32
        ) * (1.0 / math.sqrt(HEAD_DIM))
        scores = jnp.where(allowed, scores, -jnp.inf)
        exponent = jnp.exp(scores - jnp.max(scores, axis=-1, keepdims=True))
        p = (exponent * (1.0 / jnp.sum(exponent, axis=-1, keepdims=True))).astype(bf16)
        probs[g] = p
        dv = lax.dot_general(p, heads(g_ref, g), (((0,), (0,)), ((), ())), preferred_element_type=f32)
        dvp[:, cols] = dv[:T].astype(bf16)
        dvo[:, cols] = dv[T:]
    dv_copy = send(dvp, dvr, nb_s.at[3], nb_r.at[3], prev_dev)

    v_copy.wait()
    for g in range(KV_HEADS):
        cols = slice(g * HEAD_DIM, (g + 1) * HEAD_DIM)
        vals = jnp.concatenate([vprev[:, cols], v_ref[:, cols]], axis=0)
        out = jnp.dot(probs[g], vals, preferred_element_type=f32).astype(bf16)
        for h in range(GROUP):
            att[:, (g * GROUP + h) * HEAD_DIM:(g * GROUP + h + 1) * HEAD_DIM] = out[h * T:(h + 1) * T]

    for p in range(DP):
        slot = jnp.zeros((brow, att.shape[1]), bf16)
        for i in range(blocks):
            weight = jnp.where(plan_ref[0, i] == p, 1.0, 0.0).astype(f32)
            slot = slot + att[i * brow:(i + 1) * brow, :] * jnp.full((1, 1), weight, f32).astype(bf16)
        slots[p] = slot

    dv_copy.wait()
    gvg[0, 0] = (dvo[...] + dvr[...].astype(f32)).astype(bf16)
    gv_copies = {}
    for c, k in [(1, 0)] + [(0, k) for k in range(1, X)]:
        gv_copies[c, k] = send(gvg.at[0, 0], gvg.at[c, k], gv_s.at[c, k], gv_r.at[c, k], {"dp": dp_to(c, k)})

    a_copies = {}
    for c, k in dp_peers:
        a_copies[c, k] = send(
            slots.at[dp_to(c, k)], arr.at[c, k], a_s.at[c, k], a_r.at[c, k], {"dp": dp_to(c, k)}
        )

    def accumulate(members, first=False, last=False):
        for b in range(NB):
            rows = slice(b * LANES, (b + 1) * LANES)
            part = None if first else yown[b]
            for c, k in members:
                term = jnp.dot(xg[c, k, rows, :], gvg[c, k], preferred_element_type=f32)
                part = term if part is None else part + term
            yown[b] = part
            if last:
                for r in range(R):
                    ysend[r, b * CH:(b + 1) * CH, :] = part[r * CH:(r + 1) * CH].astype(bf16)

    x_copies[1, 0].wait_recv()
    gv_copies[1, 0].wait_recv()
    accumulate([(0, 0), (1, 0)], first=True, last=X == 1)
    nearest = sorted(range(1, X), key=lambda k: min(k, X - k))
    for k in nearest:
        gv_copies[0, k].wait_recv()
        gv_copies[1, k] = send(gvg.at[0, k], gvg.at[1, k], gf_s.at[k], gf_r.at[k], {"dp": dp_to(1, 0)})
    for k in nearest:
        x_copies[0, k].wait_recv()
        x_copies[1, k].wait_recv()
    if X > 1:
        accumulate([(0, k) for k in nearest])
        for k in nearest:
            gv_copies[1, k].wait_recv()
        accumulate([(1, k) for k in nearest], last=True)
    y_copies = [
        send(ysend.at[(rep + j) % R], yrecv.at[j], y_s.at[j], y_r.at[j], {"rep": (rep + j) % R})
        for j in range(1, R)
    ]
    for copy in y_copies:
        copy.wait_recv()
    for b in range(NB):
        total = yown[b, pl.ds(pl.multiple_of(rep * CH, CH), CH), :]
        for j in range(1, R):
            total = total + yrecv[j, b * CH:(b + 1) * CH, :].astype(f32)
        for cc in range(CC):
            for w in range(W // LANES):
                zf[b * CC + cc, w * JJ:(w + 1) * JJ, :] = total[
                    cc * JJ:(cc + 1) * JJ, w * LANES:(w + 1) * LANES
                ]
    zsend[...] = zf[...].astype(bf16)
    z_copies = [
        send(zsend.at[(ctx + j) % C], zrecv.at[j], z_s.at[j], z_r.at[j], {"ctx": (ctx + j) % C})
        for j in range(1, C)
    ]

    for c, k in dp_peers:
        p_copies[c, k].wait_recv()
        a_copies[c, k].wait_recv()
    arr[0, 0] = slots[dp]
    planall[0, 0] = planrow[...]
    for i in range(blocks):
        result = jnp.zeros((brow, att.shape[1]), bf16)
        for c in range(2):
            for k in range(X):
                weight = jnp.where(planall[c, k][:, i:i + 1] == dp, 1.0, 0.0).astype(bf16)
                result = result + arr[c, k] * weight
        placed_ref[i * brow:(i + 1) * brow, :] = result
    store = pltpu.make_async_copy(placed_ref, placed_hbm, out_s)
    store.start()

    for copy in z_copies:
        copy.wait_recv()
    total = zf[ctx]
    for j in range(1, C):
        total = total + zrecv[j].astype(f32)
    full[dp, rep] = total.astype(bf16)
    ay_copies = [
        send(full.at[dp, rep], full.at[dp, rep], ay_s.at[j], ay_r.at[j], {"rep": (rep + j) % R})
        for j in range(1, R)
    ]
    ad_copies = []
    for j in [0] + sorted(range(1, R), key=lambda j: min(j, R - j)):
        if j:
            ay_copies[j - 1].wait_recv()
        piece = full.at[dp, (rep + R - j) % R]
        for c, k in dp_peers:
            ad_copies.append(
                send(piece, piece, ad_s.at[j, c, k], ad_r.at[j, c, k], {"dp": dp_to(c, k)})
            )
    for copy in ad_copies:
        copy.wait_recv()
    for d in range(DP):
        for r in range(R):
            for w in range(W // LANES):
                wg_ref[d * U + r * JJ:d * U + (r + 1) * JJ, w * LANES:(w + 1) * LANES] = full[
                    d, r, w * JJ:(w + 1) * JJ, :
                ].astype(f32)
    store.wait()
    for group in (x_copies, p_copies, a_copies, gv_copies):
        for copy in group.values():
            copy.wait_send()
    for copy in y_copies + z_copies + ay_copies + ad_copies:
        copy.wait_send()


def local(inputs, queries, keys, values, grad_out, doc_ids, plan):
    DP, C, R = lax.axis_size("dp"), lax.axis_size("ctx"), lax.axis_size("rep")
    X = DP // 2
    T, D = inputs.shape[1:]
    QW, W = queries.shape[2], keys.shape[2]
    blocks = plan.shape[1]
    U = D // (DP * C)
    JJ, CC = U // R, LANES // U
    NB, rows = C // CC, C * U
    brow = T // blocks
    zrow = JJ * (W // LANES)
    bf16, f32, i32 = jnp.bfloat16, jnp.float32, jnp.int32
    vmem = pltpu.VMEM
    dma = pltpu.SemaphoreType.DMA
    spec = pl.BlockSpec(memory_space=pltpu.VMEM)

    def body(*refs):
        kernel((DP, C, R), *refs)

    placed, weight_grad = pl.pallas_call(
        body,
        out_shape=(jax.ShapeDtypeStruct((T, QW), bf16), jax.ShapeDtypeStruct((D // C, W), f32)),
        in_specs=[pl.BlockSpec(memory_space=pltpu.HBM)] * 5 + [spec] + [pl.BlockSpec(memory_space=pltpu.SMEM)],
        out_specs=(pl.BlockSpec(memory_space=pltpu.HBM), spec),
        scratch_shapes=[
            vmem((T, QW), bf16),
            vmem((T, D), bf16),
            vmem((T, QW), bf16),
            vmem((T, W), bf16),
            vmem((T, W), bf16),
            vmem((T, QW), bf16),
            vmem((DP, LANES, CC * DP * U), bf16),
            vmem((DP, rows, T), bf16),
            vmem((2, X, rows, T), bf16),
            vmem((T, W), bf16),
            vmem((T, W), bf16),
            vmem((1, T), i32),
            vmem((KV_HEADS, GROUP * T, 2 * T), bf16),
            vmem((T, W), bf16),
            vmem((T, W), f32),
            vmem((T, W), bf16),
            vmem((2, X, T, W), bf16),
            vmem((T, QW), bf16),
            vmem((DP, brow, QW), bf16),
            vmem((2, X, brow, QW), bf16),
            vmem((1, LANES), i32),
            vmem((2, X, 1, LANES), i32),
            vmem((R, C * JJ, W), bf16),
            vmem((NB, LANES, W), f32),
            vmem((R, C * JJ, W), bf16),
            vmem((C, zrow, LANES), f32),
            vmem((C, zrow, LANES), bf16),
            vmem((C, zrow, LANES), bf16),
            vmem((DP, R, zrow, LANES), bf16),
            dma((4,)), dma((4,)),
            dma((2, X)), dma((2, X)),
            dma((2, X)), dma((2, X)),
            dma((X,)), dma((X,)),
            dma((2, X)), dma((2, X)),
            dma((2, X)), dma((2, X)),
            dma((R,)), dma((R,)),
            dma((C,)), dma((C,)),
            dma((R,)), dma((R,)),
            dma((R, 2, X)), dma((R, 2, X)),
            dma((5,)), dma,
        ],
        compiler_params=pltpu.CompilerParams(
            collective_id=0, has_side_effects=True, vmem_limit_bytes=67_000_000
        ),
    )(inputs[0], queries[0], keys[0], values[0], grad_out[0], doc_ids, plan)
    return (placed[None], weight_grad)


def solution(mesh):
    tokens = P("dp", ("ctx", "rep"), None)
    marks = P("dp", ("ctx", "rep"))
    return jax.shard_map(
        local,
        mesh=mesh,
        in_specs=(tokens, tokens, tokens, tokens, tokens, marks, marks),
        out_specs=(tokens, P("ctx", None)),
        check_vma=False,
    )
```

```python
import math

import jax
import jax.numpy as jnp
from jax import lax
from jax.experimental import pallas as pl
from jax.experimental.pallas import tpu as pltpu
from jax.sharding import PartitionSpec as P

HEAD_DIM = 128
KV_HEADS = 4
GROUP = 4
LANES = 128
MESH = pl.DeviceIdType.MESH


def kernel(
    sizes,
    x_hbm, q_hbm, k_hbm, v_hbm, g_hbm, docs_ref, plan_ref,
    placed_hbm, wg_ref,
    placed_ref, x_ref, q_ref, k_ref, v_ref, g_ref, perm, xs, xg, kprev, vprev, docprev, probs, dvp, dvo, dvr, gvg, att, slots, arr,
    planrow, planall, ysend, yown, yrecv, zf, zsend, zrecv, zbf, zbsend, zbrecv, ybf, ybrecv, full,
    nb_s, nb_r, x_s, x_r, gv_s, gv_r, gf_s, gf_r, a_s, a_r, p_s, p_r,
    y_s, y_r, z_s, z_r, ay_s, ay_r, ad_s, ad_r, zb_s, zb_r, yb_s, yb_r, in_s, out_s,
):
    DP, C, R = sizes
    X = DP // 2
    T, D = x_hbm.shape
    W = k_hbm.shape[1]
    blocks = plan_ref.shape[1]
    brow = T // blocks
    U = D // (DP * C)
    JJ = U // R
    CC = LANES // U
    NB = C // CC
    CH = CC * JJ
    WA = W - LANES
    ZA = JJ * (WA // LANES)
    f32, bf16 = jnp.float32, jnp.bfloat16

    dp, ctx, rep = lax.axis_index("dp"), lax.axis_index("ctx"), lax.axis_index("rep")
    chip, core = dp // 2, dp % 2
    shard = ctx * R + rep
    after, before = (shard + 1) % (C * R), (shard + C * R - 1) % (C * R)
    next_dev = {"ctx": after // R, "rep": after % R}
    prev_dev = {"ctx": before // R, "rep": before % R}

    def dp_to(c, k):
        return ((chip + k) % X) * 2 + (core + c) % 2

    dp_peers = [(c, k) for c in range(2) for k in range(X) if (c, k) != (0, 0)]

    barrier = pltpu.get_barrier_semaphore()

    def greet(device):
        pl.semaphore_signal(barrier, inc=1, device_id=device, device_id_type=MESH)

    greet(next_dev)
    greet(prev_dev)
    for c, k in dp_peers:
        greet({"dp": dp_to(c, k)})
    for j in range(1, R):
        greet({"rep": (rep + j) % R})
    for j in range(1, C):
        greet({"ctx": (ctx + j) % C})

    loads = [
        pltpu.make_async_copy(src, dst, in_s.at[i])
        for i, (src, dst) in enumerate(
            [(k_hbm, k_ref), (x_hbm, x_ref), (v_hbm, v_ref), (q_hbm, q_ref), (g_hbm, g_ref)]
        )
    ]
    for load in loads:
        load.start()

    def send(src, dst, ssem, rsem, device):
        copy = pltpu.make_async_remote_copy(
            src_ref=src, dst_ref=dst, send_sem=ssem, recv_sem=rsem, device_id=device, device_id_type=MESH
        )
        copy.start()
        return copy

    lane = lax.broadcasted_iota(jnp.int32, (1, LANES), 1)
    row = jnp.zeros((1, LANES), jnp.int32)
    for i in range(blocks):
        row = jnp.where(lane == i, plan_ref[0, i], row)
    planrow[...] = row

    zf[...] = jnp.zeros_like(zf)
    ybf[...] = jnp.zeros_like(ybf)
    width = CC * DP * U
    for d in range(DP):
        o = lax.broadcasted_iota(jnp.int32, (LANES, 1), 0)
        rr, cc, jj = o // CH, (o % CH) // JJ, o % JJ
        source = cc * (DP * U) + d * U + rr * JJ + jj
        column = lax.broadcasted_iota(jnp.int32, (LANES, width), 1)
        perm[d] = jnp.where(column == source, 1.0, 0.0).astype(bf16)

    for load in loads:
        load.wait()
    for b in range(NB):
        for d in range(DP):
            xs[d, b * LANES:(b + 1) * LANES, :] = lax.dot_general(
                perm[d], x_ref[:, b * width:(b + 1) * width], (((1,), (1,)), ((), ())),
                preferred_element_type=f32,
            ).astype(bf16)
    pl.semaphore_wait(barrier, 2 + (DP - 1) + (R - 1) + (C - 1))

    near = [
        send(k_ref, kprev, nb_s.at[0], nb_r.at[0], next_dev),
        send(docs_ref, docprev, nb_s.at[2], nb_r.at[2], next_dev),
    ]
    v_copy = send(v_ref, vprev, nb_s.at[1], nb_r.at[1], next_dev)

    x_copies, p_copies = {}, {}
    for c, k in dp_peers:
        to = {"dp": dp_to(c, k)}
        p_copies[c, k] = send(planrow, planall.at[c, k], p_s.at[c, k], p_r.at[c, k], to)
        x_copies[c, k] = send(xs.at[dp_to(c, k)], xg.at[c, k], x_s.at[c, k], x_r.at[c, k], to)
    xg[0, 0] = xs[dp]

    docs = docs_ref[...].astype(f32)
    by_row = jnp.broadcast_to(docs, (T, T)).T
    u_pos = lax.broadcasted_iota(jnp.int32, (T, T), 1)
    t_pos = lax.broadcasted_iota(jnp.int32, (T, T), 0)
    own = jnp.where((by_row == docs) & (u_pos <= t_pos), 1.0, 0.0)
    for copy in near:
        copy.wait()
    prior = jnp.where(by_row == docprev[...].astype(f32), 1.0, 0.0) * jnp.where(shard > 0, 1.0, 0.0)
    allowed = jnp.concatenate([prior, own], axis=1)
    allowed = jnp.concatenate([allowed] * GROUP, axis=0) > 0.5

    def heads(ref, g):
        return jnp.concatenate(
            [ref[:, (g * GROUP + h) * HEAD_DIM:(g * GROUP + h + 1) * HEAD_DIM] for h in range(GROUP)], axis=0
        )

    for g in range(KV_HEADS):
        cols = slice(g * HEAD_DIM, (g + 1) * HEAD_DIM)
        keys = jnp.concatenate([kprev[:, cols], k_ref[:, cols]], axis=0)
        scores = lax.dot_general(
            heads(q_ref, g), keys, (((1,), (1,)), ((), ())), preferred_element_type=f32
        ) * (1.0 / math.sqrt(HEAD_DIM))
        scores = jnp.where(allowed, scores, -jnp.inf)
        exponent = jnp.exp(scores - jnp.max(scores, axis=-1, keepdims=True))
        p = (exponent * (1.0 / jnp.sum(exponent, axis=-1, keepdims=True))).astype(bf16)
        probs[g] = p
        dv = lax.dot_general(p, heads(g_ref, g), (((0,), (0,)), ((), ())), preferred_element_type=f32)
        dvp[:, cols] = dv[:T].astype(bf16)
        dvo[:, cols] = dv[T:]
    dv_copy = send(dvp, dvr, nb_s.at[3], nb_r.at[3], prev_dev)

    v_copy.wait()
    for g in range(KV_HEADS):
        cols = slice(g * HEAD_DIM, (g + 1) * HEAD_DIM)
        vals = jnp.concatenate([vprev[:, cols], v_ref[:, cols]], axis=0)
        out = jnp.dot(probs[g], vals, preferred_element_type=f32).astype(bf16)
        for h in range(GROUP):
            att[:, (g * GROUP + h) * HEAD_DIM:(g * GROUP + h + 1) * HEAD_DIM] = out[h * T:(h + 1) * T]

    for p in range(DP):
        slot = jnp.zeros((brow, att.shape[1]), bf16)
        for i in range(blocks):
            weight = jnp.where(plan_ref[0, i] == p, 1.0, 0.0).astype(f32)
            slot = slot + att[i * brow:(i + 1) * brow, :] * jnp.full((1, 1), weight, f32).astype(bf16)
        slots[p] = slot

    dv_copy.wait()
    gvg[0, 0] = (dvo[...] + dvr[...].astype(f32)).astype(bf16)
    gv_copies = {}
    for c, k in [(1, 0)] + [(0, k) for k in range(1, X)]:
        gv_copies[c, k] = send(gvg.at[0, 0], gvg.at[c, k], gv_s.at[c, k], gv_r.at[c, k], {"dp": dp_to(c, k)})

    a_copies = {}
    for c, k in dp_peers:
        a_copies[c, k] = send(
            slots.at[dp_to(c, k)], arr.at[c, k], a_s.at[c, k], a_r.at[c, k], {"dp": dp_to(c, k)}
        )

    def accumulate(members, first=False, last=False):
        for b in range(NB):
            rows = slice(b * LANES, (b + 1) * LANES)
            part = None if first else yown[b]
            for c, k in members:
                term = jnp.dot(xg[c, k, rows, :], gvg[c, k], preferred_element_type=f32)
                part = term if part is None else part + term
            yown[b] = part
            if last:
                for r in range(R):
                    ysend[r, b * CH:(b + 1) * CH, :] = part[r * CH:(r + 1) * CH, :WA].astype(bf16)
                    for cc in range(CC):
                        zbf[b * CC + cc, r * JJ:(r + 1) * JJ, :] = part[
                            r * CH + cc * JJ:r * CH + (cc + 1) * JJ, WA:
                        ]

    x_copies[1, 0].wait_recv()
    gv_copies[1, 0].wait_recv()
    accumulate([(0, 0), (1, 0)], first=True, last=X == 1)
    nearest = sorted(range(1, X), key=lambda k: min(k, X - k))
    for k in nearest:
        gv_copies[0, k].wait_recv()
        gv_copies[1, k] = send(gvg.at[0, k], gvg.at[1, k], gf_s.at[k], gf_r.at[k], {"dp": dp_to(1, 0)})
    for k in nearest:
        x_copies[0, k].wait_recv()
        x_copies[1, k].wait_recv()
    if X > 1:
        accumulate([(0, k) for k in nearest])
        for k in nearest:
            gv_copies[1, k].wait_recv()
        accumulate([(1, k) for k in nearest], last=True)
    y_copies = [
        send(ysend.at[(rep + j) % R], yrecv.at[j], y_s.at[j], y_r.at[j], {"rep": (rep + j) % R})
        for j in range(1, R)
    ]
    zbsend[...] = zbf[...].astype(bf16)
    zb_copies = [
        send(zbsend.at[(ctx + j) % C], zbrecv.at[j], zb_s.at[j], zb_r.at[j], {"ctx": (ctx + j) % C})
        for j in range(1, C)
    ]
    for copy in y_copies:
        copy.wait_recv()
    for b in range(NB):
        total = yown[b, pl.ds(pl.multiple_of(rep * CH, CH), CH), :WA]
        for j in range(1, R):
            total = total + yrecv[j, b * CH:(b + 1) * CH, :].astype(f32)
        for cc in range(CC):
            for w in range(WA // LANES):
                zf[b * CC + cc, w * JJ:(w + 1) * JJ, :] = total[
                    cc * JJ:(cc + 1) * JJ, w * LANES:(w + 1) * LANES
                ]
    zsend[...] = zf[...].astype(bf16)
    z_copies = [
        send(zsend.at[(ctx + j) % C], zrecv.at[j], z_s.at[j], z_r.at[j], {"ctx": (ctx + j) % C})
        for j in range(1, C)
    ]

    for copy in zb_copies:
        copy.wait_recv()
    total = zbf[ctx]
    for j in range(1, C):
        total = total + zbrecv[j].astype(f32)
    for r in range(R):
        ybf[r, :JJ, :] = total[r * JJ:(r + 1) * JJ]
    yb_copies = [
        send(ybf.at[(rep + j) % R], ybrecv.at[j], yb_s.at[j], yb_r.at[j], {"rep": (rep + j) % R})
        for j in range(1, R)
    ]
    for c, k in dp_peers:
        p_copies[c, k].wait_recv()
        a_copies[c, k].wait_recv()
    arr[0, 0] = slots[dp]
    planall[0, 0] = planrow[...]
    for i in range(blocks):
        result = jnp.zeros((brow, att.shape[1]), bf16)
        for c in range(2):
            for k in range(X):
                weight = jnp.where(planall[c, k][:, i:i + 1] == dp, 1.0, 0.0).astype(bf16)
                result = result + arr[c, k] * weight
        placed_ref[i * brow:(i + 1) * brow, :] = result
    store = pltpu.make_async_copy(placed_ref, placed_hbm, out_s)
    store.start()

    for copy in z_copies:
        copy.wait_recv()
    total = zf[ctx]
    for j in range(1, C):
        total = total + zrecv[j].astype(f32)
    for copy in yb_copies:
        copy.wait_recv()
    total_b = ybf[rep]
    for j in range(1, R):
        total_b = total_b + ybrecv[j]
    full[dp, rep] = jnp.concatenate([total[:ZA], total_b[:JJ]], axis=0).astype(bf16)
    ay_copies = [
        send(full.at[dp, rep], full.at[dp, rep], ay_s.at[j], ay_r.at[j], {"rep": (rep + j) % R})
        for j in range(1, R)
    ]
    ad_copies = []
    for j in [0] + sorted(range(1, R), key=lambda j: min(j, R - j)):
        if j:
            ay_copies[j - 1].wait_recv()
        piece = full.at[dp, (rep + R - j) % R]
        for c, k in dp_peers:
            ad_copies.append(
                send(piece, piece, ad_s.at[j, c, k], ad_r.at[j, c, k], {"dp": dp_to(c, k)})
            )
    for copy in ad_copies:
        copy.wait_recv()
    for d in range(DP):
        for r in range(R):
            for w in range(W // LANES):
                wg_ref[d * U + r * JJ:d * U + (r + 1) * JJ, w * LANES:(w + 1) * LANES] = full[
                    d, r, w * JJ:(w + 1) * JJ, :
                ].astype(f32)
    store.wait()
    for group in (x_copies, p_copies, a_copies, gv_copies):
        for copy in group.values():
            copy.wait_send()
    for copy in y_copies + z_copies + zb_copies + yb_copies + ay_copies + ad_copies:
        copy.wait_send()


def local(inputs, queries, keys, values, grad_out, doc_ids, plan):
    DP, C, R = lax.axis_size("dp"), lax.axis_size("ctx"), lax.axis_size("rep")
    X = DP // 2
    T, D = inputs.shape[1:]
    QW, W = queries.shape[2], keys.shape[2]
    blocks = plan.shape[1]
    U = D // (DP * C)
    JJ, CC = U // R, LANES // U
    NB, rows = C // CC, C * U
    brow = T // blocks
    zrow = JJ * (W // LANES)
    bf16, f32, i32 = jnp.bfloat16, jnp.float32, jnp.int32
    vmem = pltpu.VMEM
    dma = pltpu.SemaphoreType.DMA
    spec = pl.BlockSpec(memory_space=pltpu.VMEM)

    def body(*refs):
        kernel((DP, C, R), *refs)

    placed, weight_grad = pl.pallas_call(
        body,
        out_shape=(jax.ShapeDtypeStruct((T, QW), bf16), jax.ShapeDtypeStruct((D // C, W), f32)),
        in_specs=[pl.BlockSpec(memory_space=pltpu.HBM)] * 5 + [spec] + [pl.BlockSpec(memory_space=pltpu.SMEM)],
        out_specs=(pl.BlockSpec(memory_space=pltpu.HBM), spec),
        scratch_shapes=[
            vmem((T, QW), bf16),
            vmem((T, D), bf16),
            vmem((T, QW), bf16),
            vmem((T, W), bf16),
            vmem((T, W), bf16),
            vmem((T, QW), bf16),
            vmem((DP, LANES, CC * DP * U), bf16),
            vmem((DP, rows, T), bf16),
            vmem((2, X, rows, T), bf16),
            vmem((T, W), bf16),
            vmem((T, W), bf16),
            vmem((1, T), i32),
            vmem((KV_HEADS, GROUP * T, 2 * T), bf16),
            vmem((T, W), bf16),
            vmem((T, W), f32),
            vmem((T, W), bf16),
            vmem((2, X, T, W), bf16),
            vmem((T, QW), bf16),
            vmem((DP, brow, QW), bf16),
            vmem((2, X, brow, QW), bf16),
            vmem((1, LANES), i32),
            vmem((2, X, 1, LANES), i32),
            vmem((R, C * JJ, W - LANES), bf16),
            vmem((NB, LANES, W), f32),
            vmem((R, C * JJ, W - LANES), bf16),
            vmem((C, zrow, LANES), f32),
            vmem((C, zrow, LANES), bf16),
            vmem((C, zrow, LANES), bf16),
            vmem((C, U, LANES), f32),
            vmem((C, U, LANES), bf16),
            vmem((C, U, LANES), bf16),
            vmem((R, max(JJ, 8), LANES), f32),
            vmem((R, max(JJ, 8), LANES), f32),
            vmem((DP, R, zrow, LANES), bf16),
            dma((4,)), dma((4,)),
            dma((2, X)), dma((2, X)),
            dma((2, X)), dma((2, X)),
            dma((X,)), dma((X,)),
            dma((2, X)), dma((2, X)),
            dma((2, X)), dma((2, X)),
            dma((R,)), dma((R,)),
            dma((C,)), dma((C,)),
            dma((R,)), dma((R,)),
            dma((R, 2, X)), dma((R, 2, X)),
            dma((C,)), dma((C,)),
            dma((R,)), dma((R,)),
            dma((5,)), dma,
        ],
        compiler_params=pltpu.CompilerParams(
            collective_id=0, has_side_effects=True, vmem_limit_bytes=67_000_000
        ),
    )(inputs[0], queries[0], keys[0], values[0], grad_out[0], doc_ids, plan)
    return (placed[None], weight_grad)


def solution(mesh):
    tokens = P("dp", ("ctx", "rep"), None)
    marks = P("dp", ("ctx", "rep"))
    return jax.shard_map(
        local,
        mesh=mesh,
        in_specs=(tokens, tokens, tokens, tokens, tokens, marks, marks),
        out_specs=(tokens, P("ctx", None)),
        check_vma=False,
    )
```

```python
import math

import jax
import jax.numpy as jnp
from jax import lax
from jax.experimental import pallas as pl
from jax.experimental.pallas import tpu as pltpu
from jax.sharding import PartitionSpec as P

HEAD_DIM = 128
KV_HEADS = 4
GROUP = 4
LANES = 128
MESH = pl.DeviceIdType.MESH


def kernel(
    sizes,
    x_hbm, q_hbm, k_hbm, v_hbm, g_hbm, docs_ref, plan_ref,
    placed_hbm, wg_ref,
    placed_ref, x_ref, q_ref, k_ref, v_ref, g_ref, perm, xs, xg, kprev, vprev, docprev, probs, dvp, dvo, dvr, gvg, att, slots, arr,
    planrow, planall, ysend, yown, yrecv, zf, zsend, zrecv, zbf, zbsend, zbrecv, ybf, ybrecv, full,
    nb_s, nb_r, x_s, x_r, gv_s, gv_r, gf_s, gf_r, a_s, a_r, p_s, p_r,
    y_s, y_r, z_s, z_r, ay_s, ay_r, ad_s, ad_r, zb_s, zb_r, yb_s, yb_r, in_s, out_s, wide,
):
    DP, C, R = sizes
    X = DP // 2
    T, D = x_hbm.shape
    W = k_hbm.shape[1]
    blocks = plan_ref.shape[1]
    brow = T // blocks
    U = D // (DP * C)
    JJ = U // R
    CC = LANES // U
    NB = C // CC
    CH = CC * JJ
    WA = W - LANES
    ZA = JJ * (WA // LANES)
    f32, bf16 = jnp.float32, jnp.bfloat16

    dp, ctx, rep = lax.axis_index("dp"), lax.axis_index("ctx"), lax.axis_index("rep")
    chip, core = dp // 2, dp % 2
    shard = ctx * R + rep
    after, before = (shard + 1) % (C * R), (shard + C * R - 1) % (C * R)
    next_dev = {"ctx": after // R, "rep": after % R}
    prev_dev = {"ctx": before // R, "rep": before % R}

    def dp_to(c, k):
        return ((chip + k) % X) * 2 + (core + c) % 2

    dp_peers = [(c, k) for c in range(2) for k in range(X) if (c, k) != (0, 0)]

    barrier = pltpu.get_barrier_semaphore()

    def greet(device):
        pl.semaphore_signal(barrier, inc=1, device_id=device, device_id_type=MESH)

    greet(next_dev)
    greet(prev_dev)
    for c, k in dp_peers:
        greet({"dp": dp_to(c, k)})
    near_rep, near_ctx = sorted({1 % R, R - 1} - {0}), sorted({1 % C, C - 1} - {0})
    for j in near_rep:
        greet({"rep": (rep + j) % R})
    for j in near_ctx:
        greet({"ctx": (ctx + j) % C})

    def widen(step):
        for i, (axis, at, n) in enumerate((("rep", rep, R), ("ctx", ctx, C))):
            reach = 2 ** step
            if 2 * reach < n:
                for j in (reach, n - reach):
                    pl.semaphore_signal(
                        wide.at[i, step], inc=1, device_id={axis: (at + j) % n}, device_id_type=MESH
                    )

    def widened(step):
        for i, n in enumerate((R, C)):
            if 2 * 2 ** step < n:
                pl.semaphore_wait(wide.at[i, step], 2)

    loads = [
        pltpu.make_async_copy(src, dst, in_s.at[i])
        for i, (src, dst) in enumerate(
            [(k_hbm, k_ref), (x_hbm, x_ref), (v_hbm, v_ref), (q_hbm, q_ref), (g_hbm, g_ref)]
        )
    ]
    for load in loads:
        load.start()

    def send(src, dst, ssem, rsem, device):
        copy = pltpu.make_async_remote_copy(
            src_ref=src, dst_ref=dst, send_sem=ssem, recv_sem=rsem, device_id=device, device_id_type=MESH
        )
        copy.start()
        return copy

    lane = lax.broadcasted_iota(jnp.int32, (1, LANES), 1)
    row = jnp.zeros((1, LANES), jnp.int32)
    for i in range(blocks):
        row = jnp.where(lane == i, plan_ref[0, i], row)
    planrow[...] = row

    zf[...] = jnp.zeros_like(zf)
    ybf[...] = jnp.zeros_like(ybf)
    width = CC * DP * U
    for d in range(DP):
        o = lax.broadcasted_iota(jnp.int32, (LANES, 1), 0)
        rr, cc, jj = o // CH, (o % CH) // JJ, o % JJ
        source = cc * (DP * U) + d * U + rr * JJ + jj
        column = lax.broadcasted_iota(jnp.int32, (LANES, width), 1)
        perm[d] = jnp.where(column == source, 1.0, 0.0).astype(bf16)

    for load in loads:
        load.wait()
    for b in range(NB):
        for d in range(DP):
            xs[d, b * LANES:(b + 1) * LANES, :] = lax.dot_general(
                perm[d], x_ref[:, b * width:(b + 1) * width], (((1,), (1,)), ((), ())),
                preferred_element_type=f32,
            ).astype(bf16)
    pl.semaphore_wait(barrier, 2 + (DP - 1) + len(near_rep) + len(near_ctx))

    near = [
        send(k_ref, kprev, nb_s.at[0], nb_r.at[0], next_dev),
        send(docs_ref, docprev, nb_s.at[2], nb_r.at[2], next_dev),
    ]
    v_copy = send(v_ref, vprev, nb_s.at[1], nb_r.at[1], next_dev)

    x_copies, p_copies = {}, {}
    for c, k in dp_peers:
        to = {"dp": dp_to(c, k)}
        p_copies[c, k] = send(planrow, planall.at[c, k], p_s.at[c, k], p_r.at[c, k], to)
        x_copies[c, k] = send(xs.at[dp_to(c, k)], xg.at[c, k], x_s.at[c, k], x_r.at[c, k], to)
    xg[0, 0] = xs[dp]
    widen(0)

    docs = docs_ref[...].astype(f32)
    by_row = jnp.broadcast_to(docs, (T, T)).T
    u_pos = lax.broadcasted_iota(jnp.int32, (T, T), 1)
    t_pos = lax.broadcasted_iota(jnp.int32, (T, T), 0)
    own = jnp.where((by_row == docs) & (u_pos <= t_pos), 1.0, 0.0)
    for copy in near:
        copy.wait()
    widened(0)
    widen(1)
    prior = jnp.where(by_row == docprev[...].astype(f32), 1.0, 0.0) * jnp.where(shard > 0, 1.0, 0.0)
    allowed = jnp.concatenate([prior, own], axis=1)
    allowed = jnp.concatenate([allowed] * GROUP, axis=0) > 0.5

    def heads(ref, g):
        return jnp.concatenate(
            [ref[:, (g * GROUP + h) * HEAD_DIM:(g * GROUP + h + 1) * HEAD_DIM] for h in range(GROUP)], axis=0
        )

    dv_copies = []
    for g in range(KV_HEADS):
        cols = slice(g * HEAD_DIM, (g + 1) * HEAD_DIM)
        keys = jnp.concatenate([kprev[:, cols], k_ref[:, cols]], axis=0)
        scores = lax.dot_general(
            heads(q_ref, g), keys, (((1,), (1,)), ((), ())), preferred_element_type=f32
        ) * (1.0 / math.sqrt(HEAD_DIM))
        scores = jnp.where(allowed, scores, -jnp.inf)
        exponent = jnp.exp(scores - jnp.max(scores, axis=-1, keepdims=True))
        p = (exponent * (1.0 / jnp.sum(exponent, axis=-1, keepdims=True))).astype(bf16)
        probs[g] = p
        dv = lax.dot_general(p, heads(g_ref, g), (((0,), (0,)), ((), ())), preferred_element_type=f32)
        dvp[:, cols] = dv[:T].astype(bf16)
        dvo[:, cols] = dv[T:]
        if g % 2:
            pair = pl.ds((g - 1) * HEAD_DIM, 2 * HEAD_DIM)
            dv_copies.append(
                send(dvp.at[:, pair], dvr.at[:, pair], nb_s.at[3 + g // 2], nb_r.at[3 + g // 2], prev_dev)
            )
    widened(1)
    widen(2)

    v_copy.wait()
    for g in range(KV_HEADS):
        cols = slice(g * HEAD_DIM, (g + 1) * HEAD_DIM)
        vals = jnp.concatenate([vprev[:, cols], v_ref[:, cols]], axis=0)
        out = jnp.dot(probs[g], vals, preferred_element_type=f32).astype(bf16)
        for h in range(GROUP):
            att[:, (g * GROUP + h) * HEAD_DIM:(g * GROUP + h + 1) * HEAD_DIM] = out[h * T:(h + 1) * T]

    for p in range(DP):
        slot = jnp.zeros((brow, att.shape[1]), bf16)
        for i in range(blocks):
            weight = jnp.where(plan_ref[0, i] == p, 1.0, 0.0).astype(f32)
            slot = slot + att[i * brow:(i + 1) * brow, :] * jnp.full((1, 1), weight, f32).astype(bf16)
        slots[p] = slot

    for copy in dv_copies:
        copy.wait()
    gvg[0, 0] = (dvo[...] + dvr[...].astype(f32)).astype(bf16)
    gv_copies = {}
    for c, k in [(1, 0)] + [(0, k) for k in range(1, X)]:
        gv_copies[c, k] = send(gvg.at[0, 0], gvg.at[c, k], gv_s.at[c, k], gv_r.at[c, k], {"dp": dp_to(c, k)})

    a_copies = {}
    for c, k in dp_peers:
        a_copies[c, k] = send(
            slots.at[dp_to(c, k)], arr.at[c, k], a_s.at[c, k], a_r.at[c, k], {"dp": dp_to(c, k)}
        )

    widened(2)

    def accumulate(members, first=False, last=False):
        for b in range(NB):
            rows = slice(b * LANES, (b + 1) * LANES)
            part = None if first else yown[b]
            for c, k in members:
                term = jnp.dot(xg[c, k, rows, :], gvg[c, k], preferred_element_type=f32)
                part = term if part is None else part + term
            yown[b] = part
            if last:
                for r in range(R):
                    ysend[r, b * CH:(b + 1) * CH, :] = part[r * CH:(r + 1) * CH, :WA].astype(bf16)
                    for cc in range(CC):
                        zbf[b * CC + cc, r * JJ:(r + 1) * JJ, :] = part[
                            r * CH + cc * JJ:r * CH + (cc + 1) * JJ, WA:
                        ]

    x_copies[1, 0].wait_recv()
    gv_copies[1, 0].wait_recv()
    accumulate([(0, 0), (1, 0)], first=True, last=X == 1)
    nearest = sorted(range(1, X), key=lambda k: min(k, X - k))
    for k in nearest:
        gv_copies[0, k].wait_recv()
        gv_copies[1, k] = send(gvg.at[0, k], gvg.at[1, k], gf_s.at[k], gf_r.at[k], {"dp": dp_to(1, 0)})
    for k in nearest:
        x_copies[0, k].wait_recv()
        x_copies[1, k].wait_recv()
    if X > 1:
        accumulate([(0, k) for k in nearest])
        for k in nearest:
            gv_copies[1, k].wait_recv()
        accumulate([(1, k) for k in nearest], last=True)
    y_copies = [
        send(ysend.at[(rep + j) % R], yrecv.at[j], y_s.at[j], y_r.at[j], {"rep": (rep + j) % R})
        for j in range(1, R)
    ]
    zbsend[...] = zbf[...].astype(bf16)
    zb_copies = [
        send(zbsend.at[(ctx + j) % C], zbrecv.at[j], zb_s.at[j], zb_r.at[j], {"ctx": (ctx + j) % C})
        for j in range(1, C)
    ]
    for copy in y_copies:
        copy.wait_recv()
    for b in range(NB):
        total = yown[b, pl.ds(pl.multiple_of(rep * CH, CH), CH), :WA]
        for j in range(1, R):
            total = total + yrecv[j, b * CH:(b + 1) * CH, :].astype(f32)
        for cc in range(CC):
            for w in range(WA // LANES):
                zf[b * CC + cc, w * JJ:(w + 1) * JJ, :] = total[
                    cc * JJ:(cc + 1) * JJ, w * LANES:(w + 1) * LANES
                ]
    zsend[...] = zf[...].astype(bf16)
    z_copies = [
        send(zsend.at[(ctx + j) % C], zrecv.at[j], z_s.at[j], z_r.at[j], {"ctx": (ctx + j) % C})
        for j in range(1, C)
    ]

    for copy in zb_copies:
        copy.wait_recv()
    total = zbf[ctx]
    for j in range(1, C):
        total = total + zbrecv[j].astype(f32)
    for r in range(R):
        ybf[r, :JJ, :] = total[r * JJ:(r + 1) * JJ]
    yb_copies = [
        send(ybf.at[(rep + j) % R], ybrecv.at[j], yb_s.at[j], yb_r.at[j], {"rep": (rep + j) % R})
        for j in range(1, R)
    ]
    for c, k in dp_peers:
        p_copies[c, k].wait_recv()
        a_copies[c, k].wait_recv()
    arr[0, 0] = slots[dp]
    planall[0, 0] = planrow[...]
    for i in range(blocks):
        result = jnp.zeros((brow, att.shape[1]), bf16)
        for c in range(2):
            for k in range(X):
                weight = jnp.where(planall[c, k][:, i:i + 1] == dp, 1.0, 0.0).astype(bf16)
                result = result + arr[c, k] * weight
        placed_ref[i * brow:(i + 1) * brow, :] = result
    store = pltpu.make_async_copy(placed_ref, placed_hbm, out_s)
    store.start()

    for copy in z_copies:
        copy.wait_recv()
    total = zf[ctx]
    for j in range(1, C):
        total = total + zrecv[j].astype(f32)
    for copy in yb_copies:
        copy.wait_recv()
    total_b = ybf[rep]
    for j in range(1, R):
        total_b = total_b + ybrecv[j]
    full[dp, rep] = jnp.concatenate([total[:ZA], total_b[:JJ]], axis=0).astype(bf16)
    ay_copies = [
        send(full.at[dp, rep], full.at[dp, rep], ay_s.at[j], ay_r.at[j], {"rep": (rep + j) % R})
        for j in range(1, R)
    ]
    ad_copies = []
    for j in [0] + sorted(range(1, R), key=lambda j: min(j, R - j)):
        if j:
            ay_copies[j - 1].wait_recv()
        piece = full.at[dp, (rep + R - j) % R]
        for c, k in dp_peers:
            ad_copies.append(
                send(piece, piece, ad_s.at[j, c, k], ad_r.at[j, c, k], {"dp": dp_to(c, k)})
            )
    for copy in ad_copies:
        copy.wait_recv()
    for d in range(DP):
        for r in range(R):
            for w in range(W // LANES):
                wg_ref[d * U + r * JJ:d * U + (r + 1) * JJ, w * LANES:(w + 1) * LANES] = full[
                    d, r, w * JJ:(w + 1) * JJ, :
                ].astype(f32)
    store.wait()
    for group in (x_copies, p_copies, a_copies, gv_copies):
        for copy in group.values():
            copy.wait_send()
    for copy in y_copies + z_copies + zb_copies + yb_copies + ay_copies + ad_copies:
        copy.wait_send()


def local(inputs, queries, keys, values, grad_out, doc_ids, plan):
    DP, C, R = lax.axis_size("dp"), lax.axis_size("ctx"), lax.axis_size("rep")
    X = DP // 2
    T, D = inputs.shape[1:]
    QW, W = queries.shape[2], keys.shape[2]
    blocks = plan.shape[1]
    U = D // (DP * C)
    JJ, CC = U // R, LANES // U
    NB, rows = C // CC, C * U
    brow = T // blocks
    zrow = JJ * (W // LANES)
    bf16, f32, i32 = jnp.bfloat16, jnp.float32, jnp.int32
    vmem = pltpu.VMEM
    dma = pltpu.SemaphoreType.DMA
    spec = pl.BlockSpec(memory_space=pltpu.VMEM)

    def body(*refs):
        kernel((DP, C, R), *refs)

    placed, weight_grad = pl.pallas_call(
        body,
        out_shape=(jax.ShapeDtypeStruct((T, QW), bf16), jax.ShapeDtypeStruct((D // C, W), f32)),
        in_specs=[pl.BlockSpec(memory_space=pltpu.HBM)] * 5 + [spec] + [pl.BlockSpec(memory_space=pltpu.SMEM)],
        out_specs=(pl.BlockSpec(memory_space=pltpu.HBM), spec),
        scratch_shapes=[
            vmem((T, QW), bf16),
            vmem((T, D), bf16),
            vmem((T, QW), bf16),
            vmem((T, W), bf16),
            vmem((T, W), bf16),
            vmem((T, QW), bf16),
            vmem((DP, LANES, CC * DP * U), bf16),
            vmem((DP, rows, T), bf16),
            vmem((2, X, rows, T), bf16),
            vmem((T, W), bf16),
            vmem((T, W), bf16),
            vmem((1, T), i32),
            vmem((KV_HEADS, GROUP * T, 2 * T), bf16),
            vmem((T, W), bf16),
            vmem((T, W), f32),
            vmem((T, W), bf16),
            vmem((2, X, T, W), bf16),
            vmem((T, QW), bf16),
            vmem((DP, brow, QW), bf16),
            vmem((2, X, brow, QW), bf16),
            vmem((1, LANES), i32),
            vmem((2, X, 1, LANES), i32),
            vmem((R, C * JJ, W - LANES), bf16),
            vmem((NB, LANES, W), f32),
            vmem((R, C * JJ, W - LANES), bf16),
            vmem((C, zrow, LANES), f32),
            vmem((C, zrow, LANES), bf16),
            vmem((C, zrow, LANES), bf16),
            vmem((C, U, LANES), f32),
            vmem((C, U, LANES), bf16),
            vmem((C, U, LANES), bf16),
            vmem((R, max(JJ, 8), LANES), f32),
            vmem((R, max(JJ, 8), LANES), f32),
            vmem((DP, R, zrow, LANES), bf16),
            dma((5,)), dma((5,)),
            dma((2, X)), dma((2, X)),
            dma((2, X)), dma((2, X)),
            dma((X,)), dma((X,)),
            dma((2, X)), dma((2, X)),
            dma((2, X)), dma((2, X)),
            dma((R,)), dma((R,)),
            dma((C,)), dma((C,)),
            dma((R,)), dma((R,)),
            dma((R, 2, X)), dma((R, 2, X)),
            dma((C,)), dma((C,)),
            dma((R,)), dma((R,)),
            dma((5,)), dma,
            pltpu.SemaphoreType.REGULAR((2, 3)),
        ],
        compiler_params=pltpu.CompilerParams(
            collective_id=0, has_side_effects=True, vmem_limit_bytes=67_000_000
        ),
    )(inputs[0], queries[0], keys[0], values[0], grad_out[0], doc_ids, plan)
    return (placed[None], weight_grad)


def solution(mesh):
    tokens = P("dp", ("ctx", "rep"), None)
    marks = P("dp", ("ctx", "rep"))
    return jax.shard_map(
        local,
        mesh=mesh,
        in_specs=(tokens, tokens, tokens, tokens, tokens, marks, marks),
        out_specs=(tokens, P("ctx", None)),
        check_vma=False,
    )
```

```python
import math

import jax
import jax.numpy as jnp
from jax import lax
from jax.experimental import pallas as pl
from jax.experimental.pallas import tpu as pltpu
from jax.sharding import PartitionSpec as P

HEAD_DIM = 128
KV_HEADS = 4
GROUP = 4
LANES = 128
MESH = pl.DeviceIdType.MESH


def kernel(
    sizes,
    x_hbm, q_hbm, k_hbm, v_hbm, g_hbm, docs_ref, plan_ref,
    placed_hbm, wg_ref,
    placed_ref, x_ref, q_ref, k_ref, v_ref, g_ref, perm, xs, xg, kprev, vprev, docprev, probs, dvp, dvo, dvr, gvg, att, slots, arr,
    planrow, planall, ysend, yown, yrecv, zf, zsend, zrecv, zbf, zbsend, zbrecv, ybf, ybrecv, full,
    nb_s, nb_r, x_s, x_r, gv_s, gv_r, gf_s, gf_r, a_s, a_r, p_s, p_r,
    y_s, y_r, z_s, z_r, ay_s, ay_r, ad_s, ad_r, zb_s, zb_r, yb_s, yb_r, in_s, out_s, wide,
):
    DP, C, R = sizes
    X = DP // 2
    T, D = x_hbm.shape
    W = k_hbm.shape[1]
    blocks = plan_ref.shape[1]
    brow = T // blocks
    U = D // (DP * C)
    JJ = U // R
    CC = LANES // U
    NB = C // CC
    CH = CC * JJ
    WA = W - LANES
    ZA = JJ * (WA // LANES)
    f32, bf16 = jnp.float32, jnp.bfloat16

    dp, ctx, rep = lax.axis_index("dp"), lax.axis_index("ctx"), lax.axis_index("rep")
    chip, core = dp // 2, dp % 2
    shard = ctx * R + rep
    after, before = (shard + 1) % (C * R), (shard + C * R - 1) % (C * R)
    next_dev = {"ctx": after // R, "rep": after % R}
    prev_dev = {"ctx": before // R, "rep": before % R}

    def dp_to(c, k):
        return ((chip + k) % X) * 2 + (core + c) % 2

    def far_first(n):
        return sorted(range(1, n), key=lambda j: -min(j, n - j))

    dp_peers = [(c, k) for k in far_first(X) + [0] for c in range(2) if (c, k) != (0, 0)]

    barrier = pltpu.get_barrier_semaphore()

    def greet(device):
        pl.semaphore_signal(barrier, inc=1, device_id=device, device_id_type=MESH)

    greet(next_dev)
    greet(prev_dev)
    for c, k in dp_peers:
        greet({"dp": dp_to(c, k)})
    near_rep, near_ctx = sorted({1 % R, R - 1} - {0}), sorted({1 % C, C - 1} - {0})
    for j in near_rep:
        greet({"rep": (rep + j) % R})
    for j in near_ctx:
        greet({"ctx": (ctx + j) % C})

    def widen(step):
        for i, (axis, at, n) in enumerate((("rep", rep, R), ("ctx", ctx, C))):
            reach = 2 ** step
            if 2 * reach < n:
                for j in (reach, n - reach):
                    pl.semaphore_signal(
                        wide.at[i, step], inc=1, device_id={axis: (at + j) % n}, device_id_type=MESH
                    )

    def widened(step):
        for i, n in enumerate((R, C)):
            if 2 * 2 ** step < n:
                pl.semaphore_wait(wide.at[i, step], 2)

    loads = [
        pltpu.make_async_copy(src, dst, in_s.at[i])
        for i, (src, dst) in enumerate(
            [(k_hbm, k_ref), (x_hbm, x_ref), (v_hbm, v_ref), (q_hbm, q_ref), (g_hbm, g_ref)]
        )
    ]
    for load in loads:
        load.start()

    def send(src, dst, ssem, rsem, device):
        copy = pltpu.make_async_remote_copy(
            src_ref=src, dst_ref=dst, send_sem=ssem, recv_sem=rsem, device_id=device, device_id_type=MESH
        )
        copy.start()
        return copy

    lane = lax.broadcasted_iota(jnp.int32, (1, LANES), 1)
    row = jnp.zeros((1, LANES), jnp.int32)
    for i in range(blocks):
        row = jnp.where(lane == i, plan_ref[0, i], row)
    planrow[...] = row

    zf[...] = jnp.zeros_like(zf)
    ybf[...] = jnp.zeros_like(ybf)
    width = CC * DP * U
    for d in range(DP):
        o = lax.broadcasted_iota(jnp.int32, (LANES, 1), 0)
        rr, cc, jj = o // CH, (o % CH) // JJ, o % JJ
        source = cc * (DP * U) + d * U + rr * JJ + jj
        column = lax.broadcasted_iota(jnp.int32, (LANES, width), 1)
        perm[d] = jnp.where(column == source, 1.0, 0.0).astype(bf16)

    for load in loads:
        load.wait()
    for b in range(NB):
        for d in range(DP):
            xs[d, b * LANES:(b + 1) * LANES, :] = lax.dot_general(
                perm[d], x_ref[:, b * width:(b + 1) * width], (((1,), (1,)), ((), ())),
                preferred_element_type=f32,
            ).astype(bf16)
    pl.semaphore_wait(barrier, 2 + (DP - 1) + len(near_rep) + len(near_ctx))

    near = [
        send(k_ref, kprev, nb_s.at[0], nb_r.at[0], next_dev),
        send(docs_ref, docprev, nb_s.at[2], nb_r.at[2], next_dev),
    ]
    v_copy = send(v_ref, vprev, nb_s.at[1], nb_r.at[1], next_dev)

    x_copies, p_copies = {}, {}
    for c, k in dp_peers:
        to = {"dp": dp_to(c, k)}
        p_copies[c, k] = send(planrow, planall.at[c, k], p_s.at[c, k], p_r.at[c, k], to)
        x_copies[c, k] = send(xs.at[dp_to(c, k)], xg.at[c, k], x_s.at[c, k], x_r.at[c, k], to)
    xg[0, 0] = xs[dp]
    widen(0)

    docs = docs_ref[...].astype(f32)
    by_row = jnp.broadcast_to(docs, (T, T)).T
    u_pos = lax.broadcasted_iota(jnp.int32, (T, T), 1)
    t_pos = lax.broadcasted_iota(jnp.int32, (T, T), 0)
    own = jnp.where((by_row == docs) & (u_pos <= t_pos), 1.0, 0.0)
    for copy in near:
        copy.wait()
    widened(0)
    widen(1)
    prior = jnp.where(by_row == docprev[...].astype(f32), 1.0, 0.0) * jnp.where(shard > 0, 1.0, 0.0)
    allowed = jnp.concatenate([prior, own], axis=1)
    allowed = jnp.concatenate([allowed] * GROUP, axis=0) > 0.5

    def heads(ref, g):
        return jnp.concatenate(
            [ref[:, (g * GROUP + h) * HEAD_DIM:(g * GROUP + h + 1) * HEAD_DIM] for h in range(GROUP)], axis=0
        )

    dv_copies = []
    for g in range(KV_HEADS):
        cols = slice(g * HEAD_DIM, (g + 1) * HEAD_DIM)
        keys = jnp.concatenate([kprev[:, cols], k_ref[:, cols]], axis=0)
        scores = lax.dot_general(
            heads(q_ref, g), keys, (((1,), (1,)), ((), ())), preferred_element_type=f32
        ) * (1.0 / math.sqrt(HEAD_DIM))
        scores = jnp.where(allowed, scores, -jnp.inf)
        exponent = jnp.exp(scores - jnp.max(scores, axis=-1, keepdims=True))
        p = (exponent * (1.0 / jnp.sum(exponent, axis=-1, keepdims=True))).astype(bf16)
        probs[g] = p
        dv = lax.dot_general(p, heads(g_ref, g), (((0,), (0,)), ((), ())), preferred_element_type=f32)
        dvp[:, cols] = dv[:T].astype(bf16)
        dvo[:, cols] = dv[T:]
        if g % 2:
            pair = pl.ds((g - 1) * HEAD_DIM, 2 * HEAD_DIM)
            dv_copies.append(
                send(dvp.at[:, pair], dvr.at[:, pair], nb_s.at[3 + g // 2], nb_r.at[3 + g // 2], prev_dev)
            )
    widened(1)
    widen(2)

    v_copy.wait()
    for g in range(KV_HEADS):
        cols = slice(g * HEAD_DIM, (g + 1) * HEAD_DIM)
        vals = jnp.concatenate([vprev[:, cols], v_ref[:, cols]], axis=0)
        out = jnp.dot(probs[g], vals, preferred_element_type=f32).astype(bf16)
        for h in range(GROUP):
            att[:, (g * GROUP + h) * HEAD_DIM:(g * GROUP + h + 1) * HEAD_DIM] = out[h * T:(h + 1) * T]

    for p in range(DP):
        slot = jnp.zeros((brow, att.shape[1]), bf16)
        for i in range(blocks):
            weight = jnp.where(plan_ref[0, i] == p, 1.0, 0.0).astype(f32)
            slot = slot + att[i * brow:(i + 1) * brow, :] * jnp.full((1, 1), weight, f32).astype(bf16)
        slots[p] = slot

    for copy in dv_copies:
        copy.wait()
    gvg[0, 0] = (dvo[...] + dvr[...].astype(f32)).astype(bf16)
    gv_copies = {}
    for c, k in [(1, 0)] + [(0, k) for k in far_first(X)]:
        gv_copies[c, k] = send(gvg.at[0, 0], gvg.at[c, k], gv_s.at[c, k], gv_r.at[c, k], {"dp": dp_to(c, k)})

    a_copies = {}
    for c, k in dp_peers:
        a_copies[c, k] = send(
            slots.at[dp_to(c, k)], arr.at[c, k], a_s.at[c, k], a_r.at[c, k], {"dp": dp_to(c, k)}
        )

    widened(2)

    def accumulate(members, first=False, last=False):
        for b in range(NB):
            rows = slice(b * LANES, (b + 1) * LANES)
            part = None if first else yown[b]
            for c, k in members:
                term = jnp.dot(xg[c, k, rows, :], gvg[c, k], preferred_element_type=f32)
                part = term if part is None else part + term
            yown[b] = part
            if last:
                for r in range(R):
                    ysend[r, b * CH:(b + 1) * CH, :] = part[r * CH:(r + 1) * CH, :WA].astype(bf16)
                    for cc in range(CC):
                        zbf[b * CC + cc, r * JJ:(r + 1) * JJ, :] = part[
                            r * CH + cc * JJ:r * CH + (cc + 1) * JJ, WA:
                        ]

    x_copies[1, 0].wait_recv()
    gv_copies[1, 0].wait_recv()
    accumulate([(0, 0), (1, 0)], first=True, last=X == 1)
    nearest = sorted(range(1, X), key=lambda k: min(k, X - k))
    for k in nearest:
        gv_copies[0, k].wait_recv()
        gv_copies[1, k] = send(gvg.at[0, k], gvg.at[1, k], gf_s.at[k], gf_r.at[k], {"dp": dp_to(1, 0)})
    for k in nearest:
        x_copies[0, k].wait_recv()
        x_copies[1, k].wait_recv()
    if X > 1:
        accumulate([(0, k) for k in nearest])
        for k in nearest:
            gv_copies[1, k].wait_recv()
        accumulate([(1, k) for k in nearest], last=True)
    y_copies = [
        send(ysend.at[(rep + j) % R], yrecv.at[j], y_s.at[j], y_r.at[j], {"rep": (rep + j) % R})
        for j in far_first(R)
    ]
    zbsend[...] = zbf[...].astype(bf16)
    zb_copies = [
        send(zbsend.at[(ctx + j) % C], zbrecv.at[j], zb_s.at[j], zb_r.at[j], {"ctx": (ctx + j) % C})
        for j in far_first(C)
    ]
    for copy in y_copies:
        copy.wait_recv()
    for b in range(NB):
        total = yown[b, pl.ds(pl.multiple_of(rep * CH, CH), CH), :WA]
        for j in range(1, R):
            total = total + yrecv[j, b * CH:(b + 1) * CH, :].astype(f32)
        for cc in range(CC):
            for w in range(WA // LANES):
                zf[b * CC + cc, w * JJ:(w + 1) * JJ, :] = total[
                    cc * JJ:(cc + 1) * JJ, w * LANES:(w + 1) * LANES
                ]
    zsend[...] = zf[...].astype(bf16)
    z_copies = [
        send(zsend.at[(ctx + j) % C], zrecv.at[j], z_s.at[j], z_r.at[j], {"ctx": (ctx + j) % C})
        for j in far_first(C)
    ]

    for copy in zb_copies:
        copy.wait_recv()
    total = zbf[ctx]
    for j in range(1, C):
        total = total + zbrecv[j].astype(f32)
    for r in range(R):
        ybf[r, :JJ, :] = total[r * JJ:(r + 1) * JJ]
    yb_copies = [
        send(ybf.at[(rep + j) % R], ybrecv.at[j], yb_s.at[j], yb_r.at[j], {"rep": (rep + j) % R})
        for j in far_first(R)
    ]
    for c, k in dp_peers:
        p_copies[c, k].wait_recv()
        a_copies[c, k].wait_recv()
    arr[0, 0] = slots[dp]
    planall[0, 0] = planrow[...]
    for i in range(blocks):
        result = jnp.zeros((brow, att.shape[1]), bf16)
        for c in range(2):
            for k in range(X):
                weight = jnp.where(planall[c, k][:, i:i + 1] == dp, 1.0, 0.0).astype(bf16)
                result = result + arr[c, k] * weight
        placed_ref[i * brow:(i + 1) * brow, :] = result
    store = pltpu.make_async_copy(placed_ref, placed_hbm, out_s)
    store.start()

    for copy in z_copies:
        copy.wait_recv()
    total = zf[ctx]
    for j in range(1, C):
        total = total + zrecv[j].astype(f32)
    for copy in yb_copies:
        copy.wait_recv()
    total_b = ybf[rep]
    for j in range(1, R):
        total_b = total_b + ybrecv[j]
    full[dp, rep] = jnp.concatenate([total[:ZA], total_b[:JJ]], axis=0).astype(bf16)
    ay_copies = [
        send(full.at[dp, rep], full.at[dp, rep], ay_s.at[j], ay_r.at[j], {"rep": (rep + j) % R})
        for j in far_first(R)
    ]
    ay_at = dict(zip(far_first(R), ay_copies))
    ad_copies = []
    for j in [0] + sorted(range(1, R), key=lambda j: min(j, R - j)):
        if j:
            ay_at[j].wait_recv()
        piece = full.at[dp, (rep + R - j) % R]
        for c, k in dp_peers:
            ad_copies.append(
                send(piece, piece, ad_s.at[j, c, k], ad_r.at[j, c, k], {"dp": dp_to(c, k)})
            )
    for copy in ad_copies:
        copy.wait_recv()
    for d in range(DP):
        for r in range(R):
            for w in range(W // LANES):
                wg_ref[d * U + r * JJ:d * U + (r + 1) * JJ, w * LANES:(w + 1) * LANES] = full[
                    d, r, w * JJ:(w + 1) * JJ, :
                ].astype(f32)
    store.wait()
    for group in (x_copies, p_copies, a_copies, gv_copies):
        for copy in group.values():
            copy.wait_send()
    for copy in y_copies + z_copies + zb_copies + yb_copies + ay_copies + ad_copies:
        copy.wait_send()


def local(inputs, queries, keys, values, grad_out, doc_ids, plan):
    DP, C, R = lax.axis_size("dp"), lax.axis_size("ctx"), lax.axis_size("rep")
    X = DP // 2
    T, D = inputs.shape[1:]
    QW, W = queries.shape[2], keys.shape[2]
    blocks = plan.shape[1]
    U = D // (DP * C)
    JJ, CC = U // R, LANES // U
    NB, rows = C // CC, C * U
    brow = T // blocks
    zrow = JJ * (W // LANES)
    bf16, f32, i32 = jnp.bfloat16, jnp.float32, jnp.int32
    vmem = pltpu.VMEM
    dma = pltpu.SemaphoreType.DMA
    spec = pl.BlockSpec(memory_space=pltpu.VMEM)

    def body(*refs):
        kernel((DP, C, R), *refs)

    placed, weight_grad = pl.pallas_call(
        body,
        out_shape=(jax.ShapeDtypeStruct((T, QW), bf16), jax.ShapeDtypeStruct((D // C, W), f32)),
        in_specs=[pl.BlockSpec(memory_space=pltpu.HBM)] * 5 + [spec] + [pl.BlockSpec(memory_space=pltpu.SMEM)],
        out_specs=(pl.BlockSpec(memory_space=pltpu.HBM), spec),
        scratch_shapes=[
            vmem((T, QW), bf16),
            vmem((T, D), bf16),
            vmem((T, QW), bf16),
            vmem((T, W), bf16),
            vmem((T, W), bf16),
            vmem((T, QW), bf16),
            vmem((DP, LANES, CC * DP * U), bf16),
            vmem((DP, rows, T), bf16),
            vmem((2, X, rows, T), bf16),
            vmem((T, W), bf16),
            vmem((T, W), bf16),
            vmem((1, T), i32),
            vmem((KV_HEADS, GROUP * T, 2 * T), bf16),
            vmem((T, W), bf16),
            vmem((T, W), f32),
            vmem((T, W), bf16),
            vmem((2, X, T, W), bf16),
            vmem((T, QW), bf16),
            vmem((DP, brow, QW), bf16),
            vmem((2, X, brow, QW), bf16),
            vmem((1, LANES), i32),
            vmem((2, X, 1, LANES), i32),
            vmem((R, C * JJ, W - LANES), bf16),
            vmem((NB, LANES, W), f32),
            vmem((R, C * JJ, W - LANES), bf16),
            vmem((C, zrow, LANES), f32),
            vmem((C, zrow, LANES), bf16),
            vmem((C, zrow, LANES), bf16),
            vmem((C, U, LANES), f32),
            vmem((C, U, LANES), bf16),
            vmem((C, U, LANES), bf16),
            vmem((R, max(JJ, 8), LANES), f32),
            vmem((R, max(JJ, 8), LANES), f32),
            vmem((DP, R, zrow, LANES), bf16),
            dma((5,)), dma((5,)),
            dma((2, X)), dma((2, X)),
            dma((2, X)), dma((2, X)),
            dma((X,)), dma((X,)),
            dma((2, X)), dma((2, X)),
            dma((2, X)), dma((2, X)),
            dma((R,)), dma((R,)),
            dma((C,)), dma((C,)),
            dma((R,)), dma((R,)),
            dma((R, 2, X)), dma((R, 2, X)),
            dma((C,)), dma((C,)),
            dma((R,)), dma((R,)),
            dma((5,)), dma,
            pltpu.SemaphoreType.REGULAR((2, 3)),
        ],
        compiler_params=pltpu.CompilerParams(
            collective_id=0, has_side_effects=True, vmem_limit_bytes=67_000_000
        ),
    )(inputs[0], queries[0], keys[0], values[0], grad_out[0], doc_ids, plan)
    return (placed[None], weight_grad)


def solution(mesh):
    tokens = P("dp", ("ctx", "rep"), None)
    marks = P("dp", ("ctx", "rep"))
    return jax.shard_map(
        local,
        mesh=mesh,
        in_specs=(tokens, tokens, tokens, tokens, tokens, marks, marks),
        out_specs=(tokens, P("ctx", None)),
        check_vma=False,
    )
```
